32 devices in a mesh: gx: 16 (over z, y, core), gy: 2 (over x).
Axes of the slice: x: 2, y: 2, z: 4, core: 2. Of those that a mesh axis runs over, the one named last changes fastest.
Arguments:
- state_field: bfloat16 [1, 64, 2048, 2048], P(None, None, 'gx', 'gy'), may hold values from -6 to 6
- spectral_x: bfloat16 [2, 32, 2, 64, 64], P(None, 'gx'), may hold values from -2 to 2
- spectral_y: bfloat16 [2, 32, 2, 64, 64], P(None, 'gy'), may hold values from -2 to 2
- expand_weight: bfloat16 [2, 64, 256], replicated, may hold values from -0.75 to 0.75
- reduce_weight: bfloat16 [2, 256, 64], replicated, may hold values from -0.375 to 0.375
Outputs:
- next_state: bfloat16 [1, 64, 2048, 2048], P(None, None, 'gx', 'gy')
The draws below stay inside these ranges and needn't reach their ends.
All inputs are finite; a program needn't handle non-finite values.
Results may differ from the reference program's by a relative error of at most 0.025.
Values may be sent and summed in bfloat16 or wider, within the bound.
A program may use at most 128 MiB of HBM per device.

```python
import jax
import jax.numpy as jnp
from jax import lax

NX = 2048
NY = 2048
CH = 64
HID = 256
MODES = 32
LAYERS = 2
ZP = 1


def shard_levels(rng, shape, shards, low, top_value):
    factor_of = 1.0
    for axis_at, blocks in shards:
        draws = jax.random.uniform(jax.random.fold_in(jax.random.fold_in(rng, 6), axis_at), (blocks,), jnp.float32, low / len(shards), top_value / len(shards))
        factor_of = factor_of * jnp.repeat(jnp.exp(draws), shape[axis_at] // blocks).reshape((-1,) + (1,) * (len(shape) - 1 - axis_at))
    return factor_of


def scatter_about(key, extent, width, reach, pieces=(), kind=jnp.bfloat16):
    values = jax.random.normal(key, extent, jnp.float32) * width
    if len(pieces) > 0:
        values = shard_levels(key, extent, pieces, -0.22, 0.18) * values
    return jnp.clip(values, min=-reach, max=reach).astype(kind)


def setup_inputs(seed: int = 0) -> dict:
    key_list = jax.random.split(jax.random.key(seed), 6)
    state_field = scatter_about(key_list[0], (ZP, CH, NX, NY), 1.0, 6.0, ((2, 16), (3, 2)))
    spectral_x = scatter_about(key_list[1], (LAYERS, MODES, 2, CH, CH), 8 ** -0.5, 2.0, ((1, 16),))
    spectral_y = scatter_about(key_list[2], (LAYERS, MODES, 2, CH, CH), 8 ** -0.5, 2.0, ((1, 2),))
    expand_weight = scatter_about(key_list[3], (LAYERS, CH, HID), CH ** -0.5, 0.75)
    reduce_weight = scatter_about(key_list[4], (LAYERS, HID, CH), HID ** -0.5, 0.375)
    return dict(state_field=state_field, spectral_x=spectral_x, spectral_y=spectral_y, expand_weight=expand_weight, reduce_weight=reduce_weight)


def make_tables(length, modes):
    positions = jnp.arange(length, dtype=jnp.int32)
    orders = jnp.arange(modes, dtype=jnp.int32)
    phase = orders[:, None] * positions[None, :] % length
    angle = 2.0 * jnp.pi * phase.astype(jnp.float32) / length
    factor = 1.0 / jnp.sqrt(jnp.float32(length))
    weight_two = jnp.where(orders == 0, 1.0, 2.0).astype(jnp.float32)[:, None]
    forward = jnp.stack([jnp.cos(angle) * factor, -jnp.sin(angle) * factor], axis=1)
    forward = forward.reshape(2 * modes, length).astype(jnp.bfloat16)
    inverse = jnp.stack([weight_two * jnp.cos(angle) * factor, -weight_two * jnp.sin(angle) * factor], axis=1)
    inverse = inverse.reshape(2 * modes, length).T.astype(jnp.bfloat16)
    return (forward, inverse)

def mix_modes(spectrum, weights):
    modes = weights.shape[0]
    shaped = spectrum.reshape((modes, 2) + spectrum.shape[1:]).astype(jnp.float32)
    weights = weights.astype(jnp.float32)
    real_in, imag_in = (shaped[:, 0], shaped[:, 1])
    real_w, imag_w = (weights[:, 0], weights[:, 1])

    def contract_modes(left, right):
        return jnp.einsum('koi,kzin->kzon', left, right)
    real_out = contract_modes(real_w, real_in) - contract_modes(imag_w, imag_in)
    imag_out = contract_modes(real_w, imag_in) + contract_modes(imag_w, real_in)
    joined = jnp.stack([real_out, imag_out], axis=1).astype(jnp.bfloat16)
    return joined.reshape(spectrum.shape)

def reference(state_field, spectral_x, spectral_y, expand_weight, reduce_weight):
    forward_x, inverse_x = make_tables(NX, MODES)
    forward_y, inverse_y = make_tables(NY, MODES)
    state = state_field
    block_rows = 128
    for layer_index in range(LAYERS):
        state_wide = state.astype(jnp.float32)
        spec_x = jnp.einsum('kx,zcxy->kzcy', forward_x.astype(jnp.float32), state_wide).astype(jnp.bfloat16)
        mixed_x = mix_modes(spec_x, spectral_x[layer_index])
        branch_x = jnp.einsum('xk,kzcy->zcxy', inverse_x.astype(jnp.float32), mixed_x.astype(jnp.float32)).astype(jnp.bfloat16)
        spec_y = jnp.einsum('ky,zcxy->kzcx', forward_y.astype(jnp.float32), state_wide).astype(jnp.bfloat16)
        mixed_y = mix_modes(spec_y, spectral_y[layer_index])
        branch_y = jnp.einsum('yk,kzcx->zcxy', inverse_y.astype(jnp.float32), mixed_y.astype(jnp.float32)).astype(jnp.bfloat16)
        total = (branch_x.astype(jnp.float32) + branch_y.astype(jnp.float32)).astype(jnp.bfloat16)
        expand_now = expand_weight[layer_index].astype(jnp.float32)
        reduce_now = reduce_weight[layer_index].astype(jnp.float32)
        blocks_total = jnp.moveaxis(total.reshape(ZP, CH, NX // block_rows, block_rows, NY), 2, 0)
        blocks_state = jnp.moveaxis(state.reshape(ZP, CH, NX // block_rows, block_rows, NY), 2, 0)

        def pointwise(pair):
            total_block, state_block = pair
            hidden = jax.nn.gelu(jnp.einsum('ch,zcxy->zhxy', expand_now, total_block.astype(jnp.float32)), approximate=True)
            hidden = hidden.astype(jnp.bfloat16).astype(jnp.float32)
            update = jnp.einsum('hc,zhxy->zcxy', reduce_now, hidden)
            return (state_block.astype(jnp.float32) + update).astype(jnp.bfloat16)
        result_blocks = lax.map(pointwise, (blocks_total, blocks_state))
        state = jnp.moveaxis(result_blocks, 0, 2).reshape(ZP, CH, NX, NY)
    return state
```

```python
import functools

import jax
import jax.numpy as jnp
from jax import lax
from jax.experimental import pallas as pl
from jax.experimental.pallas import tpu as pltpu
from jax.sharding import PartitionSpec as P

CHUNKS = 2
LANES = 128
PAD = 4
GELU_A = 0.7978845608028654
GELU_B = 0.044715
GELU_S = (GELU_A * GELU_B) ** (1.0 / 3.0)


def local_tables(first, count, length, modes):
    positions = first + jnp.arange(count, dtype=jnp.int32)
    orders = jnp.arange(modes, dtype=jnp.int32)
    phase = orders[:, None] * positions[None, :] % length
    angle = 2.0 * jnp.pi * phase.astype(jnp.float32) / length
    factor = 1.0 / jnp.sqrt(jnp.float32(length))
    weight_two = jnp.where(orders == 0, 1.0, 2.0).astype(jnp.float32)[:, None]
    real, imag = jnp.cos(angle) * factor, -jnp.sin(angle) * factor
    forward = jnp.stack([real, imag], axis=1).reshape(2 * modes, count)
    inverse = jnp.stack([weight_two * real, weight_two * imag], axis=1)
    inverse = inverse.reshape(2 * modes, count)
    return forward.astype(jnp.bfloat16), inverse.astype(jnp.bfloat16)


def dot(left, right):
    return jnp.dot(left, right, preferred_element_type=jnp.float32)


def group_spectra(base, news, fx, fyt, s_ref, acc_ref):
    rows2 = fx.shape[0]
    count, rows = len(news), news[0].shape[0]
    wide = dot(fx, jnp.concatenate(news, axis=1))
    for i in range(count):
        s_ref[pl.ds((base + i) * (rows2 + PAD), rows2), :] = wide[:, i * LANES : (i + 1) * LANES]
    tall = dot(jnp.concatenate(news, axis=0), fyt)
    for i in range(count):
        acc_ref[base + i] = acc_ref[base + i] + tall[i * rows : (i + 1) * rows]


def write_spectra(specx_ref, specy_ref, s_ref, acc_ref):
    rows2, channels, _ = specx_ref.shape
    for k in range(rows2):
        specx_ref[k] = s_ref[pl.ds(k, channels, stride=rows2 + PAD), :].astype(jnp.bfloat16)

    @pl.when(pl.program_id(0) == pl.num_programs(0) - 1)
    def _():
        specy_ref[...] = acc_ref[...].astype(jnp.bfloat16)


def clear_first(acc_ref):
    @pl.when(pl.program_id(0) == 0)
    def _():
        acc_ref[...] = jnp.zeros_like(acc_ref)


def first_kernel(state_ref, fx_ref, fyt_ref, specx_ref, specy_ref, s_ref, acc_ref):
    clear_first(acc_ref)
    fx, fyt = fx_ref[...], fyt_ref[...]

    @pl.loop(0, state_ref.shape[0] // 4)
    def _(g):
        base = g * 4
        group_spectra(base, [state_ref[base + i] for i in range(4)], fx, fyt, s_ref, acc_ref)

    write_spectra(specx_ref, specy_ref, s_ref, acc_ref)


def layer_kernel(last, state_ref, mixed_ref, a_ref, iy_ref, w1_ref, w2_ref, *refs):
    if last:
        out_ref, m_ref, t_ref = refs[-3:]
    else:
        fx_ref, fyt_ref, out_ref, specx_ref, specy_ref, m_ref, t_ref, s_ref, acc_ref = refs
        clear_first(acc_ref)
        fx, fyt = fx_ref[...], fyt_ref[...]
    channels, rows, _ = state_ref.shape
    rows2 = mixed_ref.shape[0]
    t_step, m_step = rows + PAD, channels + PAD
    for k in range(rows2):
        m_ref[pl.ds(k * m_step, channels), :] = mixed_ref[k].astype(jnp.float32)
    iy = iy_ref[...]

    @pl.loop(0, channels // 4)
    def _(g):
        for i in range(4):
            c = g * 4 + i
            part = m_ref[pl.ds(c, rows2, stride=m_step), :].astype(jnp.bfloat16)
            t_ref[pl.ds(c * t_step, rows), :] = dot(a_ref[c], jnp.concatenate([part, iy], axis=0))

    w1, w2 = w1_ref[...], w2_ref[...]
    cg = jnp.bfloat16(GELU_A / GELU_S)

    @pl.loop(0, rows // 8)
    def _(g):
        base = g * 8
        parts = [t_ref[pl.ds(base + i, channels, stride=t_step), :] for i in range(8)]
        h = dot(w1, jnp.concatenate(parts, axis=1).astype(jnp.bfloat16)).astype(jnp.bfloat16)
        u = dot(w2, h + h * jnp.tanh(h * (h * h + cg)))
        for i in range(8):
            t_ref[pl.ds(base + i, channels, stride=t_step), :] = u[:, i * LANES : (i + 1) * LANES]

    @pl.loop(0, channels // 4)
    def _(g):
        base = g * 4
        news = []
        for i in range(4):
            c = base + i
            new = state_ref[c].astype(jnp.float32) + t_ref[pl.ds(c * t_step, rows), :]
            new = new.astype(jnp.bfloat16)
            out_ref[c] = new
            news.append(new)
        if not last:
            group_spectra(base, news, fx, fyt, s_ref, acc_ref)

    if not last:
        write_spectra(specx_ref, specy_ref, s_ref, acc_ref)


def whole(array):
    zeros = (0,) * array.ndim
    return pl.BlockSpec(array.shape, lambda j: zeros)


def body(state_field, spectral_x, spectral_y, expand_weight, reduce_weight):
    planes, channels, rows, cols = state_field.shape
    layers, hidden = expand_weight.shape[0], expand_weight.shape[2]
    nx, ny = rows * lax.axis_size("gx"), cols * lax.axis_size("gy")
    modes = spectral_x.shape[1] * lax.axis_size("gx")
    rows2 = 2 * modes
    chunks = CHUNKS if cols % (CHUNKS * LANES) == 0 else cols // LANES
    width = cols // chunks
    steps = width // LANES
    forward_x, inverse_x = local_tables(lax.axis_index("gx") * rows, rows, nx, modes)
    forward_y, inverse_y = local_tables(lax.axis_index("gy") * cols, cols, ny, modes)
    forward_yt = forward_y.T
    inverse_xt = inverse_x.T

    def block_matrix(w):
        top = jnp.concatenate([w[..., 0, :, :], -w[..., 1, :, :]], axis=-1)
        low = jnp.concatenate([w[..., 1, :, :], w[..., 0, :, :]], axis=-1)
        return jnp.concatenate([top, low], axis=-2)

    mat_x = block_matrix(spectral_x)
    mat_y = block_matrix(lax.all_gather(spectral_y, "gy", axis=1, tiled=True))

    bf16 = jnp.bfloat16
    s_scr = pltpu.VMEM((channels * (rows2 + PAD), LANES), jnp.float32)
    m_scr = pltpu.VMEM((rows2 * (channels + PAD), LANES), jnp.float32)
    t_scr = pltpu.VMEM((channels * (rows + PAD), LANES), jnp.float32)
    acc_scr = pltpu.VMEM((channels, rows, rows2), jnp.float32)
    specx_shape = jax.ShapeDtypeStruct((rows2, channels, width), bf16)
    specx_spec = pl.BlockSpec((rows2, channels, LANES), lambda j: (0, 0, j))
    specy_shape = jax.ShapeDtypeStruct((channels, rows, rows2), bf16)
    specy_spec = pl.BlockSpec((channels, rows, rows2), lambda j: (0, 0, 0))
    params = pltpu.CompilerParams(
        dimension_semantics=("arbitrary",), vmem_limit_bytes=56 * 1024 * 1024
    )
    cells = rows * width

    def cost(flops, moved):
        return pl.CostEstimate(flops=flops, bytes_accessed=moved, transcendentals=0)

    def at(first):
        return pl.BlockSpec((channels, rows, LANES), lambda j: (0, 0, j + first))

    def fyt_spec(first):
        return pl.BlockSpec((LANES, rows2), lambda j: (j + first, 0))

    spectra_flops = 4 * rows2 * channels * cells

    def first_call(state, n):
        return pl.pallas_call(
            first_kernel,
            name="spectra",
            grid=(steps,),
            in_specs=[at(n * steps), whole(forward_x), fyt_spec(n * steps)],
            out_specs=[specx_spec, specy_spec],
            out_shape=[specx_shape, specy_shape],
            scratch_shapes=[s_scr, acc_scr],
            compiler_params=params,
            cost_estimate=cost(spectra_flops, 4 * channels * cells),
        )(state, forward_x, forward_yt)

    def layer_call(last, state, first, n, mixed, a, w1, w2, result):
        ins = [state, mixed, a, inverse_y, w1, w2]
        specs = [
            at(first),
            specx_spec,
            whole(a),
            pl.BlockSpec((rows2, LANES), lambda j: (0, j + n * steps)),
            whole(w1),
            whole(w2),
        ]
        aliases = {}
        scratch = [m_scr, t_scr]
        if last:
            out_shape = [jax.ShapeDtypeStruct((channels, rows, cols), bf16)]
            out_specs = [at(n * steps)]
            if result is not None:
                aliases = {len(ins): 0}
                ins.append(result)
                specs.append(pl.BlockSpec(memory_space=pl.ANY))
        else:
            ins += [forward_x, forward_yt]
            specs += [whole(forward_x), fyt_spec(n * steps)]
            out_shape = [jax.ShapeDtypeStruct((channels, rows, width), bf16), specx_shape, specy_shape]
            out_specs = [at(0), specx_spec, specy_spec]
            scratch += [s_scr, acc_scr]
        flops = (4 * channels * hidden * 2 + 8 * rows2 * channels) * cells
        return pl.pallas_call(
            functools.partial(layer_kernel, last),
            name="layer_last" if last else "layer",
            grid=(steps,),
            in_specs=specs,
            out_specs=out_specs,
            out_shape=out_shape,
            scratch_shapes=scratch,
            input_output_aliases=aliases,
            compiler_params=params,
            cost_estimate=cost(flops, 8 * channels * cells),
        )(*ins)

    state = state_field.reshape(channels, rows, cols)
    pieces = [(state, n * steps) for n in range(chunks)]
    spectra = [first_call(state, n) for n in range(chunks)]
    for layer in range(layers):
        last = layer == layers - 1
        owned = [lax.psum_scatter(s, "gx", scatter_dimension=0, tiled=True) for s, _ in spectra]
        mixed = []
        for part in owned:
            pairs = part.reshape(part.shape[0] // 2, 2 * channels, width)
            product = jnp.einsum(
                "moi,miy->moy", mat_x[layer], pairs, preferred_element_type=jnp.float32
            )
            product = product.astype(bf16).reshape(part.shape)
            mixed.append(lax.all_gather(product, "gx", axis=0, tiled=True))
        spec_y = sum(s.astype(jnp.float32) for _, s in spectra).astype(bf16)
        spec_y = lax.psum(jnp.transpose(spec_y, (2, 0, 1)), "gy")
        mixed_y = jnp.einsum(
            "moi,mix->mox",
            mat_y[layer],
            spec_y.reshape(modes, 2 * channels, rows),
            preferred_element_type=jnp.float32,
        ).astype(bf16)
        mixed_y = jnp.transpose(mixed_y.reshape(rows2, channels, rows), (1, 2, 0))
        a = jnp.concatenate(
            [jnp.broadcast_to(inverse_xt[None], (channels, rows, rows2)), mixed_y], axis=2
        )
        w1 = (expand_weight[layer].astype(jnp.float32) * GELU_S).astype(bf16).T
        w2 = (reduce_weight[layer].astype(jnp.float32) * (0.5 / GELU_S)).astype(bf16).T
        result, next_pieces, next_spectra = None, [], []
        for n in range(chunks):
            source, first = pieces[n]
            outs = layer_call(last, source, first, n, mixed[n], a, w1, w2, result)
            if last:
                result = outs[0]
            else:
                next_pieces.append((outs[0], 0))
                next_spectra.append((outs[1], outs[2]))
        pieces, spectra = next_pieces, next_spectra
    return result.reshape(state_field.shape)


def solution(mesh):
    in_specs = (
        P(None, None, "gx", "gy"),
        P(None, "gx", None, None, None),
        P(None, "gy", None, None, None),
        P(),
        P(),
    )
    out_specs = P(None, None, "gx", "gy")
    return jax.shard_map(body, mesh=mesh, in_specs=in_specs, out_specs=out_specs, check_vma=False)
```

```python
import functools

import jax
import jax.numpy as jnp
from jax import lax
from jax.experimental import pallas as pl
from jax.experimental.pallas import tpu as pltpu
from jax.sharding import PartitionSpec as P

LANES = 128
PAD = 4
GELU_A = 0.7978845608028654
GELU_B = 0.044715
GELU_S = (GELU_A * GELU_B) ** (1.0 / 3.0)
MESH = pl.DeviceIdType.MESH


def bit_reversed(count):
    bits = count.bit_length() - 1
    return [int(format(i, "b").zfill(bits)[::-1], 2) if bits else 0 for i in range(count)]


def mode_order(modes, owners):
    each = modes // owners
    return [o * each + j for o in bit_reversed(owners) for j in range(each)]


def local_tables(first, count, length, order):
    modes = len(order)
    positions = first + jnp.arange(count, dtype=jnp.int32)
    orders = jnp.array(order, dtype=jnp.int32)
    phase = orders[:, None] * positions[None, :] % length
    angle = 2.0 * jnp.pi * phase.astype(jnp.float32) / length
    factor = 1.0 / jnp.sqrt(jnp.float32(length))
    weight_two = jnp.where(orders == 0, 1.0, 2.0).astype(jnp.float32)[:, None]
    real, imag = jnp.cos(angle) * factor, -jnp.sin(angle) * factor
    forward = jnp.stack([real, imag], axis=1).reshape(2 * modes, count)
    inverse = jnp.stack([weight_two * real, weight_two * imag], axis=1)
    inverse = inverse.reshape(2 * modes, count)
    return forward.astype(jnp.bfloat16), inverse.astype(jnp.bfloat16)


def dot(left, right):
    return jnp.dot(left, right, preferred_element_type=jnp.float32)


def dot_nt(left, right):
    return lax.dot_general(
        left, right, (((1,), (1,)), ((), ())), preferred_element_type=jnp.float32
    )


class Exchange:
    def __init__(self, axis, size, send, full, recv, send_sem, recv_sem, mix):
        self.axis, self.size = axis, size
        self.bits = size.bit_length() - 1
        self.stages = 2 * self.bits
        self.send, self.full, self.recv = send, full, recv
        self.send_sem, self.recv_sem = send_sem, recv_sem
        self.mix = mix
        self.me = lax.axis_index(axis)

    def bit(self, s):
        return lax.rem(self.me // (1 << s), 2)

    def base(self, s):
        total = 0
        for b in range(s):
            total = total + self.bit(b) * (self.size >> (b + 1))
        return total

    def partner(self, s):
        return self.me + (1 - 2 * self.bit(s)) * (1 << s)

    def copy(self, stage, m):
        if stage < self.bits:
            half = self.size >> (stage + 1)
            start = self.base(stage) + (1 - self.bit(stage)) * half
            src = self.send.at[m, pl.ds(start, half)]
            dst = self.recv[stage].at[m]
            peer = self.partner(stage)
        else:
            s = self.stages - 1 - stage
            half = self.size >> (s + 1)
            src = self.full.at[m, pl.ds(self.base(s + 1), half)]
            dst = self.full.at[m, pl.ds(self.base(s + 1), half)]
            peer = self.partner(s)
        return pltpu.make_async_remote_copy(
            src_ref=src,
            dst_ref=dst,
            send_sem=self.send_sem.at[stage, m],
            recv_sem=self.recv_sem.at[stage, m],
            device_id={self.axis: peer},
            device_id_type=MESH,
        )

    def start(self, stage, m):
        self.copy(stage, m).start()

    def finish(self, stage, layer, m):
        self.copy(stage, m).wait()
        if stage < self.bits:
            half = self.size >> (stage + 1)
            keep = self.base(stage + 1)
            rows = self.send.shape[2]
            got = self.recv[stage]

            @pl.loop(0, half)
            def _(i):
                for r in range(rows):
                    self.send[m, keep + i, r] = self.send[m, keep + i, r] + got[m, i, r]

            if stage == self.bits - 1:
                self.mix(layer, m, self.base(self.bits))
        if stage + 1 < self.stages:
            self.start(stage + 1, m)


def mega(layers, gx, gy, state_ref, fx_ref, fy_ref, ixt_ref, iy_ref, matx_ref, maty_ref,
         w1_ref, w2_ref, out_ref, *scratch):
    scratch = list(scratch)
    st, sx, mx, sy, my, t_ref, m_ref, acc_ref, a_ref = scratch[:9]
    bits_x, bits_y = gx.bit_length() - 1, gy.bit_length() - 1
    rx = scratch[9 : 9 + bits_x]
    ry = scratch[9 + bits_x : 9 + bits_x + bits_y]
    sendx, recvx, sendy, recvy, load_sem, store_sem = scratch[9 + bits_x + bits_y :]
    chunks, channels, rows, _ = st.shape
    rows2 = fx_ref.shape[0]
    per_x, per_y = rows2 // gx, rows2 // gy
    t_step, m_step = rows + PAD, channels + PAD
    bf16, f32 = jnp.bfloat16, jnp.float32

    def mix_x(layer, m, at):
        for j in range(per_x // 2):
            pair = sx[m, at, 2 * j : 2 * j + 2].reshape(2 * channels, LANES)
            got = dot(matx_ref[layer, j], pair).astype(bf16)
            mx[m, at, 2 * j : 2 * j + 2] = got.reshape(2, channels, LANES)

    def mix_y(layer, m, at):
        @pl.loop(0, per_y // 2)
        def _(j):
            pair = sy[m, at, pl.ds(2 * j, 2)].reshape(2 * channels, rows)
            got = dot(maty_ref[layer, j], pair).astype(bf16)
            my[m, at, pl.ds(2 * j, 2)] = got.reshape(2, channels, rows)

    ex = Exchange("gx", gx, sx, mx, rx, sendx, recvx, mix_x)
    ey = Exchange("gy", gy, sy, my, ry, sendy, recvy, mix_y)

    def lanes(m):
        return pl.ds(pl.multiple_of(m * LANES, LANES), LANES)

    def load(m):
        return pltpu.make_async_copy(state_ref.at[:, :, lanes(m)], st.at[m], load_sem.at[m])

    def store(m):
        return pltpu.make_async_copy(st.at[m], out_ref.at[:, :, lanes(m)], store_sem.at[m])

    def spectra(base, news, fx, fy):
        count = len(news)
        wide = dot(fx, jnp.concatenate(news, axis=1))
        tall = dot_nt(fy, jnp.concatenate(news, axis=0))
        for i in range(count):
            at = pl.ds((base + i) * m_step, rows2)
            m_ref[at, :] = wide[:, i * LANES : (i + 1) * LANES]
            acc_ref[at, :] = acc_ref[at, :] + tall[:, i * rows : (i + 1) * rows]

    def clear(m):
        @pl.when(m == 0)
        def _():
            acc_ref[...] = jnp.zeros_like(acc_ref)

    def send_spectra(m):
        for p in range(gx):
            for r in range(per_x):
                k = p * per_x + r
                sx[m, p, r] = m_ref[pl.ds(k, channels, stride=m_step), :].astype(bf16)
        ex.start(0, m)

        @pl.when(m == chunks - 1)
        def _():
            for p in range(gy):
                for r in range(per_y):
                    k = p * per_y + r
                    sy[0, p, r] = acc_ref[pl.ds(k, channels, stride=m_step), :].astype(bf16)
            if bits_y:
                ey.start(0, 0)

    def first_task(m):
        load(m).wait()
        clear(m)
        fx, fy = fx_ref[...], fy_ref[m]

        @pl.loop(0, channels // 4)
        def _(g):
            base = g * 4
            spectra(base, [st[m, base + i] for i in range(4)], fx, fy)

        send_spectra(m)

    def build_a():
        for p in range(gy):
            for r in range(per_y):
                at = pl.ds((p * per_y + r) * m_step, channels)
                acc_ref[at, :] = my[0, p, r].astype(f32)
        top = ixt_ref[...]

        @pl.loop(0, channels)
        def _(c):
            low = acc_ref[pl.ds(c, rows2, stride=m_step), :]
            a_ref[c] = jnp.concatenate([top, low], axis=0).T.astype(bf16)

    def layer_task(layer, m):
        for p in range(gx):
            for r in range(per_x):
                at = pl.ds((p * per_x + r) * m_step, channels)
                m_ref[at, :] = mx[m, p, r].astype(f32)
        iy = iy_ref[m]

        @pl.loop(0, channels // 4)
        def _(g):
            for i in range(4):
                c = g * 4 + i
                part = m_ref[pl.ds(c, rows2, stride=m_step), :].astype(bf16)
                t_ref[pl.ds(c * t_step, rows), :] = dot(
                    a_ref[c], jnp.concatenate([part, iy], axis=0)
                )

        w1, w2 = w1_ref[layer], w2_ref[layer]
        cg = jnp.bfloat16(GELU_A / GELU_S)

        @pl.loop(0, rows // 8)
        def _(g):
            base = g * 8
            parts = [t_ref[pl.ds(base + i, channels, stride=t_step), :] for i in range(8)]
            h = dot(w1, jnp.concatenate(parts, axis=1).astype(bf16)).astype(bf16)
            u = dot(w2, h + h * jnp.tanh(h * (h * h + cg)))
            for i in range(8):
                t_ref[pl.ds(base + i, channels, stride=t_step), :] = u[
                    :, i * LANES : (i + 1) * LANES
                ]

        def updated(c):
            new = st[m, c].astype(f32) + t_ref[pl.ds(c * t_step, rows), :]
            new = new.astype(bf16)
            st[m, c] = new
            return new

        @pl.when(layer < layers - 1)
        def _():
            clear(m)
            fx, fy = fx_ref[...], fy_ref[m]

            @pl.loop(0, channels // 4)
            def _(g):
                base = g * 4
                spectra(base, [updated(base + i) for i in range(4)], fx, fy)

            send_spectra(m)

        @pl.when(layer == layers - 1)
        def _():
            @pl.loop(0, channels // 4)
            def _(g):
                for i in range(4):
                    updated(g * 4 + i)

            store(m).start()

    barrier = pltpu.get_barrier_semaphore()
    for one in (ex, ey):
        for s in range(one.bits):
            pl.semaphore_signal(
                barrier, inc=1, device_id={one.axis: one.partner(s)}, device_id_type=MESH
            )

    @pl.loop(0, chunks)
    def _(m):
        load(m).start()

    pl.semaphore_wait(barrier, ex.bits + ey.bits)

    period = max(chunks + 1, ex.stages + 1, chunks - 1 + ey.stages)
    ticks = layers * period + chunks

    @pl.loop(0, ticks)
    def _(t):
        for stage in reversed(range(ey.stages)):
            q = t - chunks - stage
            layer = q // period

            @pl.when((q >= 0) & (lax.rem(q, period) == 0) & (layer < layers))
            def _():
                ey.finish(stage, layer, 0)

        for stage in reversed(range(ex.stages)):
            q = t - 1 - stage
            layer = q // period
            m = lax.rem(q, period)

            @pl.when((q >= 0) & (m < chunks) & (layer < layers))
            def _():
                ex.finish(stage, layer, m)

        turn = t // period
        m = lax.rem(t, period)

        @pl.when(t < chunks)
        def _():
            first_task(m)

        @pl.when((turn > 0) & (m == 0))
        def _():
            build_a()

        @pl.when((turn > 0) & (m < chunks))
        def _():
            layer_task(turn - 1, m)

    @pl.loop(0, chunks)
    def _(m):
        store(m).wait()


def body(state_field, spectral_x, spectral_y, expand_weight, reduce_weight):
    planes, channels, rows, cols = state_field.shape
    layers, hidden = expand_weight.shape[0], expand_weight.shape[2]
    gx, gy = lax.axis_size("gx"), lax.axis_size("gy")
    nx, ny = rows * gx, cols * gy
    modes = spectral_x.shape[1] * gx
    rows2 = 2 * modes
    chunks = cols // LANES
    bf16, f32 = jnp.bfloat16, jnp.float32
    forward_x, inverse_x = local_tables(
        lax.axis_index("gx") * rows, rows, nx, mode_order(modes, gx)
    )
    forward_y, inverse_y = local_tables(
        lax.axis_index("gy") * cols, cols, ny, mode_order(modes, gy)
    )

    def by_chunk(table):
        return jnp.transpose(table.reshape(rows2, chunks, LANES), (1, 0, 2))

    def block_matrix(w):
        top = jnp.concatenate([w[..., 0, :, :], -w[..., 1, :, :]], axis=-1)
        low = jnp.concatenate([w[..., 1, :, :], w[..., 0, :, :]], axis=-1)
        return jnp.concatenate([top, low], axis=-2)

    w1 = jnp.swapaxes((expand_weight.astype(f32) * GELU_S).astype(bf16), 1, 2)
    w2 = jnp.swapaxes((reduce_weight.astype(f32) * (0.5 / GELU_S)).astype(bf16), 1, 2)
    args = [
        state_field.reshape(channels, rows, cols),
        forward_x,
        by_chunk(forward_y),
        inverse_x.astype(f32),
        by_chunk(inverse_y),
        block_matrix(spectral_x),
        block_matrix(spectral_y),
        w1,
        w2,
    ]
    bits_x, bits_y = gx.bit_length() - 1, gy.bit_length() - 1
    per_x, per_y = rows2 // gx, rows2 // gy
    m_rows = max(channels, rows2) * (max(channels, rows2) + PAD)
    scratch = [
        pltpu.VMEM((chunks, channels, rows, LANES), bf16),
        pltpu.VMEM((chunks, gx, per_x, channels, LANES), bf16),
        pltpu.VMEM((chunks, gx, per_x, channels, LANES), bf16),
        pltpu.VMEM((1, gy, per_y, channels, rows), bf16),
        pltpu.VMEM((1, gy, per_y, channels, rows), bf16),
        pltpu.VMEM((channels * (rows + PAD), LANES), f32),
        pltpu.VMEM((m_rows, LANES), f32),
        pltpu.VMEM((m_rows, rows), f32),
        pltpu.VMEM((channels, rows, 2 * rows2), bf16),
    ]
    for s in range(bits_x):
        scratch.append(pltpu.VMEM((chunks, gx >> (s + 1), per_x, channels, LANES), bf16))
    for s in range(bits_y):
        scratch.append(pltpu.VMEM((1, gy >> (s + 1), per_y, channels, rows), bf16))
    dma = pltpu.SemaphoreType.DMA
    scratch += [dma((2 * bits_x, chunks))] * 2 + [dma((2 * bits_y, 1))] * 2 + [dma((chunks,))] * 2
    vmem = pl.BlockSpec(memory_space=pltpu.VMEM)
    anywhere = pl.BlockSpec(memory_space=pl.ANY)
    out = pl.pallas_call(
        functools.partial(mega, layers, gx, gy),
        name="layers",
        out_shape=jax.ShapeDtypeStruct((channels, rows, cols), bf16),
        in_specs=[anywhere] + [vmem] * (len(args) - 1),
        out_specs=anywhere,
        scratch_shapes=scratch,
        compiler_params=pltpu.CompilerParams(
            collective_id=0, has_side_effects=True, vmem_limit_bytes=67043328
        ),
    )(*args)
    return out.reshape(state_field.shape)


def solution(mesh):
    in_specs = (
        P(None, None, "gx", "gy"),
        P(None, "gx", None, None, None),
        P(None, "gy", None, None, None),
        P(),
        P(),
    )
    out_specs = P(None, None, "gx", "gy")
    return jax.shard_map(body, mesh=mesh, in_specs=in_specs, out_specs=out_specs, check_vma=False)
```

```python
import functools

import jax
import jax.numpy as jnp
from jax import lax
from jax.experimental import pallas as pl
from jax.experimental.pallas import tpu as pltpu
from jax.sharding import PartitionSpec as P

LANES = 128
PAD = 4
GROUP = 8
WIDE = 16
GELU_A = 0.7978845608028654
GELU_B = 0.044715
GELU_S = (GELU_A * GELU_B) ** (1.0 / 3.0)
MESH = pl.DeviceIdType.MESH


def bit_reversed(count):
    bits = count.bit_length() - 1
    return [int(format(i, "b").zfill(bits)[::-1], 2) if bits else 0 for i in range(count)]


def mode_order(modes, owners):
    each = modes // owners
    return [o * each + j for o in bit_reversed(owners) for j in range(each)]


def local_tables(first, count, length, order):
    modes = len(order)
    positions = first + jnp.arange(count, dtype=jnp.int32)
    orders = jnp.array(order, dtype=jnp.int32)
    phase = orders[:, None] * positions[None, :] % length
    angle = 2.0 * jnp.pi * phase.astype(jnp.float32) / length
    factor = 1.0 / jnp.sqrt(jnp.float32(length))
    weight_two = jnp.where(orders == 0, 1.0, 2.0).astype(jnp.float32)[:, None]
    real, imag = jnp.cos(angle) * factor, -jnp.sin(angle) * factor
    forward = jnp.stack([real, imag], axis=1).reshape(2 * modes, count)
    inverse = jnp.stack([weight_two * real, weight_two * imag], axis=1)
    inverse = inverse.reshape(2 * modes, count)
    return forward.astype(jnp.bfloat16), inverse.astype(jnp.bfloat16)


def dot(left, right):
    return jnp.dot(left, right, preferred_element_type=jnp.float32)


def dot_nt(left, right):
    return lax.dot_general(
        left, right, (((1,), (1,)), ((), ())), preferred_element_type=jnp.float32
    )


def stage_order(stages):
    first = [0, stages - 3] if stages >= 4 else []
    last = [1, stages - 2] if stages >= 4 else []
    middle = [s for s in reversed(range(stages)) if s not in first + last]
    return list(dict.fromkeys(first + middle + last))


class Exchange:
    def __init__(self, axis, size, send, full, recv, send_sem, recv_sem, mix):
        self.axis, self.size = axis, size
        self.bits = size.bit_length() - 1
        self.stages = 2 * self.bits
        self.send, self.full, self.recv = send, full, recv
        self.send_sem, self.recv_sem = send_sem, recv_sem
        self.mix = mix
        self.me = lax.axis_index(axis)

    def bit(self, s):
        return lax.rem(self.me // (1 << s), 2)

    def base(self, s):
        total = 0
        for b in range(s):
            total = total + self.bit(b) * (self.size >> (b + 1))
        return total

    def partner(self, s):
        return self.me + (1 - 2 * self.bit(s)) * (1 << s)

    def copy(self, stage, m):
        if stage < self.bits:
            half = self.size >> (stage + 1)
            start = self.base(stage) + (1 - self.bit(stage)) * half
            src = self.send.at[m, pl.ds(start, half)]
            dst = self.recv[stage].at[m]
            peer = self.partner(stage)
        else:
            s = self.stages - 1 - stage
            half = self.size >> (s + 1)
            src = self.full.at[m, pl.ds(self.base(s + 1), half)]
            dst = self.full.at[m, pl.ds(self.base(s + 1), half)]
            peer = self.partner(s)
        return pltpu.make_async_remote_copy(
            src_ref=src,
            dst_ref=dst,
            send_sem=self.send_sem.at[stage, m],
            recv_sem=self.recv_sem.at[stage, m],
            device_id={self.axis: peer},
            device_id_type=MESH,
        )

    def start(self, stage, m):
        self.copy(stage, m).start()

    def finish(self, stage, layer, m):
        self.copy(stage, m).wait()
        if stage < self.bits:
            half = self.size >> (stage + 1)
            keep = self.base(stage + 1)
            rows = self.send.shape[2]
            got = self.recv[stage]

            @pl.loop(0, half)
            def _(i):
                for r in range(rows):
                    self.send[m, keep + i, r] = self.send[m, keep + i, r] + got[m, i, r]

            if stage == self.bits - 1:
                self.mix(layer, m, self.base(self.bits))
        if stage + 1 < self.stages:
            self.start(stage + 1, m)


def mega(layers, gx, gy, state_ref, fx_ref, fy_ref, ixt_ref, iy_ref, matx_ref, maty_ref,
         w1_ref, w2_ref, out_ref, *scratch):
    scratch = list(scratch)
    st, sx, mx, sy, my, t_ref, u_ref, h0_ref, h1_ref, m_ref, acc_ref, a_ref = scratch[:12]
    bits_x, bits_y = gx.bit_length() - 1, gy.bit_length() - 1
    rx = scratch[12 : 12 + bits_x]
    ry = scratch[12 + bits_x : 12 + bits_x + bits_y]
    sendx, recvx, sendy, recvy, load_sem, store_sem = scratch[12 + bits_x + bits_y :]
    chunks, channels, rows, _ = st.shape
    rows2 = fx_ref.shape[0]
    per_x, per_y = rows2 // gx, rows2 // gy
    t_step, m_step = rows + PAD, channels + PAD
    bf16, f32 = jnp.bfloat16, jnp.float32

    def mix_x(layer, m, at):
        for j in range(per_x // 2):
            pair = sx[m, at, 2 * j : 2 * j + 2].reshape(2 * channels, LANES)
            got = dot(matx_ref[layer, j], pair).astype(bf16)
            mx[m, at, 2 * j : 2 * j + 2] = got.reshape(2, channels, LANES)

    def mix_y(layer, m, at):
        @pl.loop(0, per_y // 2)
        def _(j):
            pair = sy[m, at, pl.ds(2 * j, 2)].reshape(2 * channels, rows)
            got = dot(maty_ref[layer, j], pair).astype(bf16)
            my[m, at, pl.ds(2 * j, 2)] = got.reshape(2, channels, rows)

    ex = Exchange("gx", gx, sx, mx, rx, sendx, recvx, mix_x)
    ey = Exchange("gy", gy, sy, my, ry, sendy, recvy, mix_y)

    def lanes(m):
        return pl.ds(pl.multiple_of(m * LANES, LANES), LANES)

    def load(m):
        return pltpu.make_async_copy(state_ref.at[:, :, lanes(m)], st.at[m], load_sem.at[m])

    def store(m):
        return pltpu.make_async_copy(st.at[m], out_ref.at[:, :, lanes(m)], store_sem.at[m])

    def spectra(base, news, fx, fy):
        count = len(news)
        wide = dot(fx, jnp.concatenate(news, axis=1))
        tall = dot_nt(fy, jnp.concatenate(news, axis=0))
        for i in range(count):
            at = pl.ds((base + i) * m_step, rows2)
            m_ref[at, :] = wide[:, i * LANES : (i + 1) * LANES]
            acc_ref[at, :] = acc_ref[at, :] + tall[:, i * rows : (i + 1) * rows]

    def clear(m):
        @pl.when(m == 0)
        def _():
            acc_ref[...] = jnp.zeros_like(acc_ref)

    def send_spectra(m):
        for p in range(gx):
            for r in range(per_x):
                k = p * per_x + r
                sx[m, p, r] = m_ref[pl.ds(k, channels, stride=m_step), :].astype(bf16)
        ex.start(0, m)

        @pl.when(m == chunks - 1)
        def _():
            for p in range(gy):
                for r in range(per_y):
                    k = p * per_y + r
                    sy[0, p, r] = acc_ref[pl.ds(k, channels, stride=m_step), :].astype(bf16)
            if bits_y:
                ey.start(0, 0)

    def first_task(m):
        load(m).wait()
        clear(m)
        fx, fy = fx_ref[...], fy_ref[m]

        @pl.loop(0, channels // WIDE)
        def _(g):
            base = g * WIDE
            spectra(base, [st[m, base + i] for i in range(WIDE)], fx, fy)

        send_spectra(m)

    def build_a():
        for p in range(gy):
            for r in range(per_y):
                at = pl.ds((p * per_y + r) * m_step, channels)
                acc_ref[at, :] = my[0, p, r].astype(f32)
        top = ixt_ref[...]

        @pl.loop(0, channels)
        def _(c):
            low = acc_ref[pl.ds(c, rows2, stride=m_step), :]
            a_ref[c] = jnp.concatenate([top, low], axis=0).T.astype(bf16)

    def layer_task(layer, m):
        for p in range(gx):
            for r in range(per_x):
                at = pl.ds((p * per_x + r) * m_step, channels)
                m_ref[at, :] = mx[m, p, r].astype(f32)
        iy = iy_ref[m]

        @pl.loop(0, channels // WIDE)
        def _(g):
            for i in range(WIDE):
                c = g * WIDE + i
                part = m_ref[pl.ds(c, rows2, stride=m_step), :].astype(bf16)
                t_ref[pl.ds(c * t_step, rows), :] = dot(
                    a_ref[c], jnp.concatenate([part, iy], axis=0)
                )

        w1, w2 = w1_ref[layer], w2_ref[layer]
        cg = jnp.bfloat16(GELU_A / GELU_S)

        def expand(base, h_ref):
            parts = [t_ref[pl.ds(base + i, channels, stride=t_step), :] for i in range(GROUP)]
            h_ref[...] = dot(w1, jnp.concatenate(parts, axis=1).astype(bf16)).astype(bf16)

        def reduce(base, h_ref):
            h = h_ref[...]
            u = dot(w2, h + h * jnp.tanh(h * (h * h + cg)))
            for i in range(GROUP):
                u_ref[pl.ds(base + i, channels, stride=t_step), :] = u[
                    :, i * LANES : (i + 1) * LANES
                ]

        expand(0, h0_ref)

        @pl.loop(0, rows // (2 * GROUP))
        def _(g):
            base = g * 2 * GROUP
            expand(base + GROUP, h1_ref)
            reduce(base, h0_ref)
            expand(lax.rem(base + 2 * GROUP, rows), h0_ref)
            reduce(base + GROUP, h1_ref)

        def updated(c):
            new = st[m, c].astype(f32) + u_ref[pl.ds(c * t_step, rows), :]
            new = new.astype(bf16)
            st[m, c] = new
            return new

        @pl.when(layer < layers - 1)
        def _():
            clear(m)
            fx, fy = fx_ref[...], fy_ref[m]

            @pl.loop(0, channels // WIDE)
            def _(g):
                base = g * WIDE
                spectra(base, [updated(base + i) for i in range(WIDE)], fx, fy)

            send_spectra(m)

        @pl.when(layer == layers - 1)
        def _():
            @pl.loop(0, channels // 4)
            def _(g):
                for i in range(4):
                    updated(g * 4 + i)

            store(m).start()

    barrier = pltpu.get_barrier_semaphore()
    for one in (ex, ey):
        for s in range(one.bits):
            pl.semaphore_signal(
                barrier, inc=1, device_id={one.axis: one.partner(s)}, device_id_type=MESH
            )

    @pl.loop(0, chunks)
    def _(m):
        load(m).start()

    pl.semaphore_wait(barrier, ex.bits + ey.bits)

    period = max(chunks + 1, ex.stages + 1, chunks - 1 + ey.stages)
    ticks = layers * period + chunks

    @pl.loop(0, ticks)
    def _(t):
        for stage in reversed(range(ey.stages)):
            q = t - chunks - stage
            layer = q // period

            @pl.when((q >= 0) & (lax.rem(q, period) == 0) & (layer < layers))
            def _():
                ey.finish(stage, layer, 0)

        for stage in stage_order(ex.stages):
            q = t - 1 - stage
            layer = q // period
            m = lax.rem(q, period)

            @pl.when((q >= 0) & (m < chunks) & (layer < layers))
            def _():
                ex.finish(stage, layer, m)

        turn = t // period
        m = lax.rem(t, period)

        @pl.when(t < chunks)
        def _():
            first_task(m)

        @pl.when((turn > 0) & (m == 0))
        def _():
            build_a()

        @pl.when((turn > 0) & (m < chunks))
        def _():
            layer_task(turn - 1, m)

    @pl.loop(0, chunks)
    def _(m):
        store(m).wait()


def body(state_field, spectral_x, spectral_y, expand_weight, reduce_weight):
    planes, channels, rows, cols = state_field.shape
    layers, hidden = expand_weight.shape[0], expand_weight.shape[2]
    gx, gy = lax.axis_size("gx"), lax.axis_size("gy")
    nx, ny = rows * gx, cols * gy
    modes = spectral_x.shape[1] * gx
    rows2 = 2 * modes
    chunks = cols // LANES
    bf16, f32 = jnp.bfloat16, jnp.float32
    forward_x, inverse_x = local_tables(
        lax.axis_index("gx") * rows, rows, nx, mode_order(modes, gx)
    )
    forward_y, inverse_y = local_tables(
        lax.axis_index("gy") * cols, cols, ny, mode_order(modes, gy)
    )

    def by_chunk(table):
        return jnp.transpose(table.reshape(rows2, chunks, LANES), (1, 0, 2))

    def block_matrix(w):
        top = jnp.concatenate([w[..., 0, :, :], -w[..., 1, :, :]], axis=-1)
        low = jnp.concatenate([w[..., 1, :, :], w[..., 0, :, :]], axis=-1)
        return jnp.concatenate([top, low], axis=-2)

    w1 = jnp.swapaxes((expand_weight.astype(f32) * GELU_S).astype(bf16), 1, 2)
    w2 = jnp.swapaxes((reduce_weight.astype(f32) * (0.5 / GELU_S)).astype(bf16), 1, 2)
    args = [
        state_field.reshape(channels, rows, cols),
        forward_x,
        by_chunk(forward_y),
        inverse_x.astype(f32),
        by_chunk(inverse_y),
        block_matrix(spectral_x),
        block_matrix(spectral_y),
        w1,
        w2,
    ]
    bits_x, bits_y = gx.bit_length() - 1, gy.bit_length() - 1
    per_x, per_y = rows2 // gx, rows2 // gy
    m_rows = max(channels, rows2) * (max(channels, rows2) + PAD)
    scratch = [
        pltpu.VMEM((chunks, channels, rows, LANES), bf16),
        pltpu.VMEM((chunks, gx, per_x, channels, LANES), bf16),
        pltpu.VMEM((chunks, gx, per_x, channels, LANES), bf16),
        pltpu.VMEM((1, gy, per_y, channels, rows), bf16),
        pltpu.VMEM((1, gy, per_y, channels, rows), bf16),
        pltpu.VMEM((channels * (rows + PAD), LANES), f32),
        pltpu.VMEM((channels * (rows + PAD), LANES), f32),
        pltpu.VMEM((hidden, GROUP * LANES), bf16),
        pltpu.VMEM((hidden, GROUP * LANES), bf16),
        pltpu.VMEM((m_rows, LANES), f32),
        pltpu.VMEM((m_rows, rows), f32),
        pltpu.VMEM((channels, rows, 2 * rows2), bf16),
    ]
    for s in range(bits_x):
        scratch.append(pltpu.VMEM((chunks, gx >> (s + 1), per_x, channels, LANES), bf16))
    for s in range(bits_y):
        scratch.append(pltpu.VMEM((1, gy >> (s + 1), per_y, channels, rows), bf16))
    dma = pltpu.SemaphoreType.DMA
    scratch += [dma((2 * bits_x, chunks))] * 2 + [dma((2 * bits_y, 1))] * 2 + [dma((chunks,))] * 2
    vmem = pl.BlockSpec(memory_space=pltpu.VMEM)
    anywhere = pl.BlockSpec(memory_space=pl.ANY)
    out = pl.pallas_call(
        functools.partial(mega, layers, gx, gy),
        name="layers",
        out_shape=jax.ShapeDtypeStruct((channels, rows, cols), bf16),
        in_specs=[anywhere] + [vmem] * (len(args) - 1),
        out_specs=anywhere,
        scratch_shapes=scratch,
        compiler_params=pltpu.CompilerParams(
            collective_id=0, has_side_effects=True, vmem_limit_bytes=67043328
        ),
    )(*args)
    return out.reshape(state_field.shape)


def solution(mesh):
    in_specs = (
        P(None, None, "gx", "gy"),
        P(None, "gx", None, None, None),
        P(None, "gy", None, None, None),
        P(),
        P(),
    )
    out_specs = P(None, None, "gx", "gy")
    return jax.shard_map(body, mesh=mesh, in_specs=in_specs, out_specs=out_specs, check_vma=False)
```

```python
import functools

import jax
import jax.numpy as jnp
from jax import lax
from jax.experimental import pallas as pl
from jax.experimental.pallas import tpu as pltpu
from jax.sharding import PartitionSpec as P

LANES = 128
PAD = 4
GROUP = 8
WIDE = 16
GELU_A = 0.7978845608028654
GELU_B = 0.044715
GELU_S = (GELU_A * GELU_B) ** (1.0 / 3.0)
MESH = pl.DeviceIdType.MESH


def bit_reversed(count):
    bits = count.bit_length() - 1
    return [int(format(i, "b").zfill(bits)[::-1], 2) if bits else 0 for i in range(count)]


def mode_order(modes, owners):
    each = modes // owners
    return [o * each + j for o in bit_reversed(owners) for j in range(each)]


def local_tables(first, count, length, order):
    rows2 = 2 * len(order)
    positions = first + jnp.arange(count, dtype=jnp.int32)
    orders = jnp.array([k for k in order for _ in range(2)], dtype=jnp.int32)[:, None]
    part = lax.broadcasted_iota(jnp.int32, (rows2, count), 0) % 2
    angle = 2.0 * jnp.pi * (orders * positions[None, :] % length).astype(jnp.float32) / length
    factor = 1.0 / jnp.sqrt(jnp.float32(length))
    forward = jnp.where(part == 0, jnp.cos(angle), -jnp.sin(angle)) * factor
    inverse = jnp.where(orders == 0, 1.0, 2.0) * forward
    return forward.astype(jnp.bfloat16), inverse.astype(jnp.bfloat16)


def dot(left, right):
    return jnp.dot(left, right, preferred_element_type=jnp.float32)


def dot_nt(left, right):
    return lax.dot_general(
        left, right, (((1,), (1,)), ((), ())), preferred_element_type=jnp.float32
    )


def stage_order(stages):
    first = [0, stages - 3] if stages >= 4 else []
    late = [1, stages - 2] if stages >= 4 else []
    middle = [s for s in reversed(range(stages - 1)) if s not in first + late]
    return list(dict.fromkeys(first + middle + late)) + [stages - 1]


class Exchange:
    def __init__(self, axis, size, send, full, recv, send_sem, recv_sem, mix):
        self.axis, self.size = axis, size
        self.bits = size.bit_length() - 1
        self.stages = 2 * self.bits
        self.send, self.full, self.recv = send, full, recv
        self.send_sem, self.recv_sem = send_sem, recv_sem
        self.mix = mix
        self.me = lax.axis_index(axis)

    def bit(self, s):
        return lax.rem(self.me // (1 << s), 2)

    def base(self, s):
        total = 0
        for b in range(s):
            total = total + self.bit(b) * (self.size >> (b + 1))
        return total

    def partner(self, s):
        return self.me + (1 - 2 * self.bit(s)) * (1 << s)

    def copy(self, stage, m):
        if stage < self.bits:
            half = self.size >> (stage + 1)
            start = self.base(stage) + (1 - self.bit(stage)) * half
            src = self.send.at[m, pl.ds(start, half)]
            dst = self.recv[stage].at[m]
            peer = self.partner(stage)
        else:
            s = self.stages - 1 - stage
            half = self.size >> (s + 1)
            src = self.full.at[m, pl.ds(self.base(s + 1), half)]
            dst = self.full.at[m, pl.ds(self.base(s + 1), half)]
            peer = self.partner(s)
        return pltpu.make_async_remote_copy(
            src_ref=src,
            dst_ref=dst,
            send_sem=self.send_sem.at[stage, m],
            recv_sem=self.recv_sem.at[stage, m],
            device_id={self.axis: peer},
            device_id_type=MESH,
        )

    def start(self, stage, m):
        self.copy(stage, m).start()

    def finish(self, stage, layer, m):
        self.copy(stage, m).wait()
        if stage < self.bits:
            half = self.size >> (stage + 1)
            keep = self.base(stage + 1)
            rows = self.send.shape[2]
            got = self.recv[stage]

            @pl.loop(0, half)
            def _(i):
                for r in range(rows):
                    self.send[m, keep + i, r] = self.send[m, keep + i, r] + got[m, i, r]

            if stage == self.bits - 1:
                self.mix(layer, m, self.base(self.bits))
        if stage + 1 < self.stages:
            self.start(stage + 1, m)


def mega(layers, gx, gy, state_ref, fx_ref, fy_ref, ixt_ref, iy_ref, spx_ref, spy_ref,
         ew_ref, rw_ref, out_ref, *scratch):
    scratch = list(scratch)
    st, sx, mx, sy, my, t_ref, u_ref, h0_ref, h1_ref, m_ref, acc_ref, a_ref = scratch[:12]
    matx_ref, maty_ref, w1_ref, w2_ref = scratch[12:16]
    bits_x, bits_y = gx.bit_length() - 1, gy.bit_length() - 1
    rx = scratch[16 : 16 + bits_x]
    ry = scratch[16 + bits_x : 16 + bits_x + bits_y]
    sendx, recvx, sendy, recvy, load_sem, store_sem = scratch[16 + bits_x + bits_y :]
    chunks, channels, rows, _ = st.shape
    rows2 = fx_ref.shape[0]
    per_x, per_y = rows2 // gx, rows2 // gy
    t_step, m_step = rows + PAD, channels + PAD
    bf16, f32 = jnp.bfloat16, jnp.float32

    def mix_x(layer, m, at):
        for j in range(per_x // 2):
            pair = sx[m, at, 2 * j : 2 * j + 2].reshape(2 * channels, LANES)
            got = dot(matx_ref[layer, j], pair).astype(bf16)
            mx[m, at, 2 * j : 2 * j + 2] = got.reshape(2, channels, LANES)

    def mix_y(layer, m, at):
        @pl.loop(0, per_y // 2)
        def _(j):
            pair = sy[m, at, pl.ds(2 * j, 2)].reshape(2 * channels, rows)
            got = dot(maty_ref[layer, j], pair).astype(bf16)
            my[m, at, pl.ds(2 * j, 2)] = got.reshape(2, channels, rows)

    ex = Exchange("gx", gx, sx, mx, rx, sendx, recvx, mix_x)
    ey = Exchange("gy", gy, sy, my, ry, sendy, recvy, mix_y)

    def prepare():
        for layer in range(layers):
            w1_ref[layer] = (ew_ref[layer].astype(f32) * GELU_S).T.astype(bf16)
            w2_ref[layer] = (rw_ref[layer].astype(f32) * (0.5 / GELU_S)).T.astype(bf16)
            for source, target in ((spx_ref, matx_ref), (spy_ref, maty_ref)):

                @pl.loop(0, source.shape[1])
                def _(j):
                    real, imag = source[layer, j, 0], source[layer, j, 1]
                    target[layer, j, :channels] = jnp.concatenate([real, -imag], axis=1)
                    target[layer, j, channels:] = jnp.concatenate([imag, real], axis=1)

    def lanes(m):
        return pl.ds(pl.multiple_of(m * LANES, LANES), LANES)

    def load(m):
        return pltpu.make_async_copy(state_ref.at[:, :, lanes(m)], st.at[m], load_sem.at[m])

    def store(m):
        return pltpu.make_async_copy(st.at[m], out_ref.at[:, :, lanes(m)], store_sem.at[m])

    def spectra(base, news, fx, fy):
        count = len(news)
        wide = dot(fx, jnp.concatenate(news, axis=1))
        tall = dot_nt(fy, jnp.concatenate(news, axis=0))
        for i in range(count):
            at = pl.ds((base + i) * m_step, rows2)
            m_ref[at, :] = wide[:, i * LANES : (i + 1) * LANES]
            acc_ref[at, :] = acc_ref[at, :] + tall[:, i * rows : (i + 1) * rows]

    def clear(m):
        @pl.when(m == 0)
        def _():
            acc_ref[...] = jnp.zeros_like(acc_ref)

    def send_spectra(m):
        for p in range(gx):
            for r in range(per_x):
                k = p * per_x + r
                sx[m, p, r] = m_ref[pl.ds(k, channels, stride=m_step), :].astype(bf16)
        ex.start(0, m)

        @pl.when(m == chunks - 1)
        def _():
            for p in range(gy):
                for r in range(per_y):
                    k = p * per_y + r
                    sy[0, p, r] = acc_ref[pl.ds(k, channels, stride=m_step), :].astype(bf16)
            if bits_y:
                ey.start(0, 0)

    def first_task(m):
        load(m).wait()
        clear(m)
        fx, fy = fx_ref[...], fy_ref[:, lanes(m)]

        @pl.loop(0, channels // WIDE)
        def _(g):
            base = g * WIDE
            spectra(base, [st[m, base + i] for i in range(WIDE)], fx, fy)

        send_spectra(m)

    def build_a():
        for p in range(gy):
            for r in range(per_y):
                at = pl.ds((p * per_y + r) * m_step, channels)
                acc_ref[at, :] = my[0, p, r].astype(f32)
        top = ixt_ref[...].astype(f32)

        @pl.loop(0, channels // 8)
        def _(g):
            for i in range(8):
                low = acc_ref[pl.ds(g * 8 + i, rows2, stride=m_step), :]
                a_ref[g * 8 + i] = jnp.concatenate([top, low], axis=0).T.astype(bf16)

    def layer_start(m):
        for p in range(gx):
            for r in range(per_x):
                at = pl.ds((p * per_x + r) * m_step, channels)
                m_ref[at, :] = mx[m, p, r].astype(f32)
        iy = iy_ref[:, lanes(m)]

        @pl.loop(0, channels // WIDE)
        def _(g):
            for i in range(WIDE):
                c = g * WIDE + i
                part = m_ref[pl.ds(c, rows2, stride=m_step), :].astype(bf16)
                t_ref[pl.ds(c * t_step, rows), :] = dot(
                    a_ref[c], jnp.concatenate([part, iy], axis=0)
                )

    def layer_rest(layer, m):
        w1, w2 = w1_ref[layer], w2_ref[layer]
        cg = jnp.bfloat16(GELU_A / GELU_S)

        def expand(base, h_ref):
            parts = [t_ref[pl.ds(base + i, channels, stride=t_step), :] for i in range(GROUP)]
            h_ref[...] = dot(w1, jnp.concatenate(parts, axis=1).astype(bf16)).astype(bf16)

        def reduce(base, h_ref):
            h = h_ref[...]
            u = dot(w2, h + h * jnp.tanh(h * (h * h + cg)))
            for i in range(GROUP):
                u_ref[pl.ds(base + i, channels, stride=t_step), :] = u[
                    :, i * LANES : (i + 1) * LANES
                ]

        expand(0, h0_ref)

        @pl.loop(0, rows // (2 * GROUP))
        def _(g):
            base = g * 2 * GROUP
            expand(base + GROUP, h1_ref)
            reduce(base, h0_ref)
            expand(lax.rem(base + 2 * GROUP, rows), h0_ref)
            reduce(base + GROUP, h1_ref)

        def updated(c):
            new = st[m, c].astype(f32) + u_ref[pl.ds(c * t_step, rows), :]
            new = new.astype(bf16)
            st[m, c] = new
            return new

        @pl.when(layer < layers - 1)
        def _():
            clear(m)
            fx, fy = fx_ref[...], fy_ref[:, lanes(m)]

            @pl.loop(0, channels // WIDE)
            def _(g):
                base = g * WIDE
                spectra(base, [updated(base + i) for i in range(WIDE)], fx, fy)

            send_spectra(m)

        @pl.when(layer == layers - 1)
        def _():
            @pl.loop(0, channels // 4)
            def _(g):
                for i in range(4):
                    updated(g * 4 + i)

            store(m).start()

    barrier = pltpu.get_barrier_semaphore()
    for one in (ex, ey):
        for s in range(one.bits):
            pl.semaphore_signal(
                barrier, inc=1, device_id={one.axis: one.partner(s)}, device_id_type=MESH
            )

    @pl.loop(0, chunks)
    def _(m):
        load(m).start()

    pl.semaphore_wait(barrier, ex.bits + ey.bits)

    prepare()
    early = pl.cdiv(chunks, 2)
    period = max(chunks, ex.stages, early + 1 + ey.stages)

    @pl.loop(0, layers * period + chunks)
    def _(t):
        turn, m = t // period, lax.rem(t, period)

        def advance(stage):
            q = t - 1 - stage
            layer, chunk = q // period, lax.rem(q, period)

            @pl.when((q >= 0) & (chunk < chunks) & (layer < layers))
            def _():
                ex.finish(stage, layer, chunk)

        if ex.stages:
            advance(ex.stages - 1)
        for stage in range(ey.stages):

            @pl.when((t == early + 1 + stage) | ((turn > 1) & (m == 0)))
            def _():
                ey.finish(stage, jnp.maximum(turn - 1, 0), 0)

        for i in range(2):

            @pl.when(2 * t + i < chunks)
            def _():
                first_task(2 * t + i)

        @pl.when((turn > 0) & (m == 0))
        def _():
            build_a()

        @pl.when((turn > 0) & (m < chunks))
        def _():
            layer_start(m)

        for stage in stage_order(ex.stages)[:-1] if ex.stages else []:
            advance(stage)

        @pl.when((turn > 0) & (m < chunks))
        def _():
            layer_rest(turn - 1, m)

    @pl.loop(0, chunks)
    def _(m):
        store(m).wait()


def body(state_field, spectral_x, spectral_y, expand_weight, reduce_weight):
    planes, channels, rows, cols = state_field.shape
    layers, hidden = expand_weight.shape[0], expand_weight.shape[2]
    gx, gy = lax.axis_size("gx"), lax.axis_size("gy")
    nx, ny = rows * gx, cols * gy
    modes = spectral_x.shape[1] * gx
    rows2 = 2 * modes
    chunks = cols // LANES
    bf16, f32 = jnp.bfloat16, jnp.float32
    own_y = spectral_y.shape[1]
    own_x = spectral_x.shape[1]
    forward_x, inverse_x = local_tables(
        lax.axis_index("gx") * rows, rows, nx, mode_order(modes, gx)
    )
    forward_y, inverse_y = local_tables(
        lax.axis_index("gy") * cols, cols, ny, mode_order(modes, gy)
    )

    args = [
        state_field.reshape(channels, rows, cols),
        forward_x,
        forward_y,
        inverse_x,
        inverse_y,
        spectral_x,
        spectral_y,
        expand_weight,
        reduce_weight,
    ]
    bits_x, bits_y = gx.bit_length() - 1, gy.bit_length() - 1
    per_x, per_y = rows2 // gx, rows2 // gy
    m_rows = max(channels, rows2) * (max(channels, rows2) + PAD)
    scratch = [
        pltpu.VMEM((chunks, channels, rows, LANES), bf16),
        pltpu.VMEM((chunks, gx, per_x, channels, LANES), bf16),
        pltpu.VMEM((chunks, gx, per_x, channels, LANES), bf16),
        pltpu.VMEM((1, gy, per_y, channels, rows), bf16),
        pltpu.VMEM((1, gy, per_y, channels, rows), bf16),
        pltpu.VMEM((channels * (rows + PAD), LANES), f32),
        pltpu.VMEM((channels * (rows + PAD), LANES), f32),
        pltpu.VMEM((hidden, GROUP * LANES), bf16),
        pltpu.VMEM((hidden, GROUP * LANES), bf16),
        pltpu.VMEM((m_rows, LANES), f32),
        pltpu.VMEM((m_rows, rows), f32),
        pltpu.VMEM((channels, rows, 2 * rows2), bf16),
        pltpu.VMEM((layers, own_x, 2 * channels, 2 * channels), bf16),
        pltpu.VMEM((layers, own_y, 2 * channels, 2 * channels), bf16),
        pltpu.VMEM((layers, hidden, channels), bf16),
        pltpu.VMEM((layers, channels, hidden), bf16),
    ]
    for s in range(bits_x):
        scratch.append(pltpu.VMEM((chunks, gx >> (s + 1), per_x, channels, LANES), bf16))
    for s in range(bits_y):
        scratch.append(pltpu.VMEM((1, gy >> (s + 1), per_y, channels, rows), bf16))
    dma = pltpu.SemaphoreType.DMA
    scratch += [dma((2 * bits_x, chunks))] * 2 + [dma((2 * bits_y, 1))] * 2 + [dma((chunks,))] * 2
    vmem = pl.BlockSpec(memory_space=pltpu.VMEM)
    anywhere = pl.BlockSpec(memory_space=pl.ANY)
    out = pl.pallas_call(
        functools.partial(mega, layers, gx, gy),
        name="layers",
        out_shape=jax.ShapeDtypeStruct((channels, rows, cols), bf16),
        in_specs=[anywhere] + [vmem] * (len(args) - 1),
        out_specs=anywhere,
        scratch_shapes=scratch,
        compiler_params=pltpu.CompilerParams(
            collective_id=0, has_side_effects=True, vmem_limit_bytes=67043328
        ),
    )(*args)
    return out.reshape(state_field.shape)


def solution(mesh):
    in_specs = (
        P(None, None, "gx", "gy"),
        P(None, "gx", None, None, None),
        P(None, "gy", None, None, None),
        P(),
        P(),
    )
    out_specs = P(None, None, "gx", "gy")
    return jax.shard_map(body, mesh=mesh, in_specs=in_specs, out_specs=out_specs, check_vma=False)
```

```python
import functools

import jax
import jax.numpy as jnp
from jax import lax
from jax.experimental import pallas as pl
from jax.experimental.pallas import tpu as pltpu
from jax.sharding import PartitionSpec as P

LANES = 128
PAD = 4
GROUP = 8
WIDE = 16
GELU_A = 0.7978845608028654
GELU_B = 0.044715
GELU_S = (GELU_A * GELU_B) ** (1.0 / 3.0)
MESH = pl.DeviceIdType.MESH


def bit_reversed(count):
    bits = count.bit_length() - 1
    return [int(format(i, "b").zfill(bits)[::-1], 2) if bits else 0 for i in range(count)]


def mode_order(modes, owners):
    each = modes // owners
    return [o * each + j for o in bit_reversed(owners) for j in range(each)]


def local_tables(first, count, length, order):
    rows2 = 2 * len(order)
    positions = first + jnp.arange(count, dtype=jnp.int32)
    orders = jnp.array([k for k in order for _ in range(2)], dtype=jnp.int32)[:, None]
    part = lax.broadcasted_iota(jnp.int32, (rows2, count), 0) % 2
    angle = 2.0 * jnp.pi * (orders * positions[None, :] % length).astype(jnp.float32) / length
    factor = 1.0 / jnp.sqrt(jnp.float32(length))
    forward = jnp.where(part == 0, jnp.cos(angle), -jnp.sin(angle)) * factor
    inverse = jnp.where(orders == 0, 1.0, 2.0) * forward
    return forward.astype(jnp.bfloat16), inverse.astype(jnp.bfloat16)


def dot(left, right):
    return jnp.dot(left, right, preferred_element_type=jnp.float32)


def dot_nt(left, right):
    return lax.dot_general(
        left, right, (((1,), (1,)), ((), ())), preferred_element_type=jnp.float32
    )


def stage_order(stages):
    first = [0, stages - 3] if stages >= 4 else []
    late = [1, stages - 2] if stages >= 4 else []
    middle = [s for s in reversed(range(stages - 1)) if s not in first + late]
    return list(dict.fromkeys(first + middle + late)) + [stages - 1]


class Exchange:
    def __init__(self, axis, size, send, full, recv, send_sem, recv_sem, mix):
        self.axis, self.size = axis, size
        self.bits = size.bit_length() - 1
        self.stages = 2 * self.bits
        self.send, self.full, self.recv = send, full, recv
        self.send_sem, self.recv_sem = send_sem, recv_sem
        self.mix = mix
        self.me = lax.axis_index(axis)

    def bit(self, s):
        return lax.rem(self.me // (1 << s), 2)

    def base(self, s):
        total = 0
        for b in range(s):
            total = total + self.bit(b) * (self.size >> (b + 1))
        return total

    def partner(self, s):
        return self.me + (1 - 2 * self.bit(s)) * (1 << s)

    def copy(self, stage, m):
        if stage < self.bits:
            half = self.size >> (stage + 1)
            start = self.base(stage) + (1 - self.bit(stage)) * half
            src = self.send.at[m, pl.ds(start, half)]
            dst = self.recv[stage].at[m]
            peer = self.partner(stage)
        else:
            s = self.stages - 1 - stage
            half = self.size >> (s + 1)
            src = self.full.at[m, pl.ds(self.base(s + 1), half)]
            dst = self.full.at[m, pl.ds(self.base(s + 1), half)]
            peer = self.partner(s)
        return pltpu.make_async_remote_copy(
            src_ref=src,
            dst_ref=dst,
            send_sem=self.send_sem.at[stage, m],
            recv_sem=self.recv_sem.at[stage, m],
            device_id={self.axis: peer},
            device_id_type=MESH,
        )

    def start(self, stage, m):
        self.copy(stage, m).start()

    def finish(self, stage, layer, m):
        self.copy(stage, m).wait()
        if stage < self.bits:
            half = self.size >> (stage + 1)
            keep = self.base(stage + 1)
            rows = self.send.shape[2]
            got = self.recv[stage]

            @pl.loop(0, half)
            def _(i):
                for r in range(rows):
                    self.send[m, keep + i, r] = self.send[m, keep + i, r] + got[m, i, r]

            if stage == self.bits - 1:
                self.mix(layer, m, self.base(self.bits))
        if stage + 1 < self.stages:
            self.start(stage + 1, m)


def transform(mixed_ref, a_ref, iy, m_ref, t_ref):
    owners, each, channels, _ = mixed_ref.shape
    rows, rows2 = a_ref.shape[1], owners * each
    t_step, m_step = rows + PAD, channels + PAD
    for p in range(owners):
        for r in range(each):
            at = pl.ds((p * each + r) * m_step, channels)
            m_ref[at, :] = mixed_ref[p, r].astype(jnp.float32)

    @pl.loop(0, channels // WIDE)
    def _(g):
        for i in range(WIDE):
            c = g * WIDE + i
            part = m_ref[pl.ds(c, rows2, stride=m_step), :].astype(jnp.bfloat16)
            t_ref[pl.ds(c * t_step, rows), :] = dot(a_ref[c], jnp.concatenate([part, iy], axis=0))


def pointwise(w1, w2, rows, t_ref, u_ref, h0_ref, h1_ref):
    channels, t_step = w2.shape[0], rows + PAD
    cg = jnp.bfloat16(GELU_A / GELU_S)

    def expand(base, h_ref):
        parts = [t_ref[pl.ds(base + i, channels, stride=t_step), :] for i in range(GROUP)]
        wide = jnp.concatenate(parts, axis=1).astype(jnp.bfloat16)
        h_ref[...] = dot(w1, wide).astype(jnp.bfloat16)

    def reduce(base, h_ref):
        h = h_ref[...]
        u = dot(w2, h + h * jnp.tanh(h * (h * h + cg)))
        for i in range(GROUP):
            u_ref[pl.ds(base + i, channels, stride=t_step), :] = u[:, i * LANES : (i + 1) * LANES]

    expand(0, h0_ref)

    @pl.loop(0, rows // (2 * GROUP))
    def _(g):
        base = g * 2 * GROUP
        expand(base + GROUP, h1_ref)
        reduce(base, h0_ref)
        expand(lax.rem(base + 2 * GROUP, rows), h0_ref)
        reduce(base + GROUP, h1_ref)


def add_update(st_ref, u_ref, c):
    rows = st_ref.shape[1]
    new = st_ref[c].astype(jnp.float32) + u_ref[pl.ds(c * (rows + PAD), rows), :]
    new = new.astype(jnp.bfloat16)
    st_ref[c] = new
    return new


def add_updates(st_ref, u_ref):
    @pl.loop(0, st_ref.shape[0] // 4)
    def _(g):
        for i in range(4):
            add_update(st_ref, u_ref, g * 4 + i)


def scaled_weights(ew, rw):
    w1 = (ew.astype(jnp.float32) * GELU_S).T.astype(jnp.bfloat16)
    return w1, (rw.astype(jnp.float32) * (0.5 / GELU_S)).astype(jnp.bfloat16)


def lanes(m):
    return pl.ds(pl.multiple_of(m * LANES, LANES), LANES)


def tail_kernel(kept, x_ref, mixed_ref, a_hbm, iy_ref, ew_ref, rw_ref, out_ref, *scratch):
    st, mx, a_ref, t_ref, u_ref, h0_ref, h1_ref, m_ref = scratch[:8]
    load_sem, mixed_sem, a_sem, store_sem = scratch[8:]
    chunks, _, rows, _ = st.shape

    def load(m):
        return pltpu.make_async_copy(x_ref.at[:, :, lanes(m)], st.at[m], load_sem.at[m])

    def store(m):
        return pltpu.make_async_copy(st.at[m], out_ref.at[:, :, lanes(m)], store_sem.at[m])

    def mixed(i):
        return pltpu.make_async_copy(mixed_ref.at[i], mx.at[i], mixed_sem.at[i])

    whole_a = pltpu.make_async_copy(a_hbm, a_ref, a_sem)
    whole_a.start()
    for i in range(chunks - kept):
        mixed(i).start()
        load(kept + i).start()
    for m in range(kept):
        load(m).start()
    w1, w2 = scaled_weights(ew_ref[...], rw_ref[...])
    whole_a.wait()

    @pl.loop(kept, chunks)
    def _(m):
        mixed(m - kept).wait()
        transform(mx.at[m - kept], a_ref, iy_ref[:, lanes(m)], m_ref, t_ref)
        pointwise(w1, w2, rows, t_ref, u_ref, h0_ref, h1_ref)
        load(m).wait()
        add_updates(st.at[m], u_ref)
        store(m).start()

        @pl.when(m == kept)
        def _():
            for other in range(kept):
                load(other).wait()
                store(other).start()

    @pl.loop(0, chunks)
    def _(m):
        store(m).wait()


def mega(layers, gx, gy, plan, state_ref, fx_ref, fy_ref, ixt_ref, iy_ref, spx_ref, spy_ref,
         ew_ref, rw_ref, out_ref, mixed_out, a_out, *scratch):
    early, period, gap, kept = plan
    scratch = list(scratch)
    st, sx, mx, sy, my, t_ref, u_ref, h0_ref, h1_ref, m_ref, acc_ref, a_ref = scratch[:12]
    matx_ref, maty_ref, w1_ref, w2_ref = scratch[12:16]
    bits_x, bits_y = gx.bit_length() - 1, gy.bit_length() - 1
    rx = scratch[16 : 16 + bits_x]
    ry = scratch[16 + bits_x : 16 + bits_x + bits_y]
    sendx, recvx, sendy, recvy, load_sem, store_sem, mixed_sem, a_sem = scratch[16 + bits_x + bits_y :]
    chunks, channels, rows, _ = st.shape
    rows2 = fx_ref.shape[0]
    per_x, per_y = rows2 // gx, rows2 // gy
    t_step, m_step = rows + PAD, channels + PAD
    bf16, f32 = jnp.bfloat16, jnp.float32

    def mix_x(layer, m, at):
        for j in range(per_x // 2):
            pair = sx[m, at, 2 * j : 2 * j + 2].reshape(2 * channels, LANES)
            got = dot(matx_ref[layer, j], pair).astype(bf16)
            mx[m, at, 2 * j : 2 * j + 2] = got.reshape(2, channels, LANES)

    def mix_y(layer, m, at):
        @pl.loop(0, per_y // 2)
        def _(j):
            pair = sy[m, at, pl.ds(2 * j, 2)].reshape(2 * channels, rows)
            got = dot(maty_ref[layer, j], pair).astype(bf16)
            my[m, at, pl.ds(2 * j, 2)] = got.reshape(2, channels, rows)

    ex = Exchange("gx", gx, sx, mx, rx, sendx, recvx, mix_x)
    ey = Exchange("gy", gy, sy, my, ry, sendy, recvy, mix_y)

    def prepare():
        for layer in range(layers):
            w1_ref[layer], w2_ref[layer] = scaled_weights(ew_ref[layer], rw_ref[layer])
            for source, target in ((spx_ref, matx_ref), (spy_ref, maty_ref)):

                @pl.loop(0, source.shape[1])
                def _(j):
                    real, imag = source[layer, j, 0], source[layer, j, 1]
                    target[layer, j, :channels] = jnp.concatenate([real, -imag], axis=1)
                    target[layer, j, channels:] = jnp.concatenate([imag, real], axis=1)

    def load(m):
        return pltpu.make_async_copy(state_ref.at[:, :, lanes(m)], st.at[m], load_sem.at[m])

    def store(m):
        return pltpu.make_async_copy(st.at[m], out_ref.at[:, :, lanes(m)], store_sem.at[m])

    def keep_mixed(i):
        return pltpu.make_async_copy(mx.at[kept + i], mixed_out.at[i], mixed_sem.at[i])

    def keep_a():
        return pltpu.make_async_copy(a_ref, a_out, a_sem)

    def spectra(base, news, fx, fy):
        count = len(news)
        wide = dot(fx, jnp.concatenate(news, axis=1))
        tall = dot_nt(fy, jnp.concatenate(news, axis=0))
        for i in range(count):
            at = pl.ds((base + i) * m_step, rows2)
            m_ref[at, :] = wide[:, i * LANES : (i + 1) * LANES]
            acc_ref[at, :] = acc_ref[at, :] + tall[:, i * rows : (i + 1) * rows]

    def clear(m):
        @pl.when(m == 0)
        def _():
            acc_ref[...] = jnp.zeros_like(acc_ref)

    def send_spectra(m):
        for p in range(gx):
            for r in range(per_x):
                k = p * per_x + r
                sx[m, p, r] = m_ref[pl.ds(k, channels, stride=m_step), :].astype(bf16)
        ex.start(0, m)

        @pl.when(m == chunks - 1)
        def _():
            for p in range(gy):
                for r in range(per_y):
                    k = p * per_y + r
                    sy[0, p, r] = acc_ref[pl.ds(k, channels, stride=m_step), :].astype(bf16)
            if bits_y:
                ey.start(0, 0)

    def first_task(m):
        load(m).wait()
        clear(m)
        fx, fy = fx_ref[...], fy_ref[:, lanes(m)]

        @pl.loop(0, channels // WIDE)
        def _(g):
            base = g * WIDE
            spectra(base, [st[m, base + i] for i in range(WIDE)], fx, fy)

        send_spectra(m)

    def build_a():
        for p in range(gy):
            for r in range(per_y):
                at = pl.ds((p * per_y + r) * m_step, channels)
                acc_ref[at, :] = my[0, p, r].astype(f32)
        top = ixt_ref[...].astype(f32)

        @pl.loop(0, channels // 8)
        def _(g):
            for i in range(8):
                low = acc_ref[pl.ds(g * 8 + i, rows2, stride=m_step), :]
                a_ref[g * 8 + i] = jnp.concatenate([top, low], axis=0).T.astype(bf16)

    def layer_start(m):
        transform(mx.at[m], a_ref, iy_ref[:, lanes(m)], m_ref, t_ref)

    def layer_rest(layer, m):
        pointwise(w1_ref[layer], w2_ref[layer], rows, t_ref, u_ref, h0_ref, h1_ref)

        @pl.when(layer < layers - 1)
        def _():
            clear(m)
            fx, fy = fx_ref[...], fy_ref[:, lanes(m)]

            @pl.loop(0, channels // WIDE)
            def _(g):
                base = g * WIDE
                spectra(base, [add_update(st.at[m], u_ref, base + i) for i in range(WIDE)], fx, fy)

            send_spectra(m)

        @pl.when((layer == layers - 2) & (m >= kept))
        def _():
            store(m).start()

        @pl.when(layer == layers - 1)
        def _():
            add_updates(st.at[m], u_ref)
            store(m).start()

    barrier = pltpu.get_barrier_semaphore()
    for one in (ex, ey):
        for s in range(one.bits):
            pl.semaphore_signal(
                barrier, inc=1, device_id={one.axis: one.partner(s)}, device_id_type=MESH
            )

    @pl.loop(0, chunks)
    def _(m):
        load(m).start()

    pl.semaphore_wait(barrier, ex.bits + ey.bits)

    prepare()
    later = period + gap

    def place(t):
        after = jnp.maximum(t - period, 0)
        turn = jnp.where(t < period, 0, 1 + after // later)
        return turn, jnp.where(t < period, t, lax.rem(after, later))

    @pl.loop(0, period + (layers - 1) * later + kept)
    def _(t):
        turn, m = place(t)

        def advance(stage):
            layer, chunk = place(t - 1 - stage)

            @pl.when((t >= 1 + stage) & (chunk < chunks) & (layer < layers))
            def _():
                ex.finish(stage, layer, chunk)
                if stage == ex.stages - 1:

                    @pl.when((layer == layers - 1) & (chunk >= kept))
                    def _():
                        keep_mixed(chunk - kept).start()

        if ex.stages:
            advance(ex.stages - 1)
        for stage in range(ey.stages):
            left = ey.stages - 1 - stage
            since = t - period + left

            @pl.when((t == period - 2 * left) | ((since >= later) & (lax.rem(since, later) == 0)))
            def _():
                ey.finish(stage, jnp.maximum(since, 0) // later, 0)

        for i in range(2):

            @pl.when(2 * t + i < chunks)
            def _():
                first_task(2 * t + i)

        @pl.when((turn > 0) & (m == 0))
        def _():
            build_a()

            @pl.when(turn == layers)
            def _():
                keep_a().start()

        @pl.when((turn > 0) & (m < chunks))
        def _():
            layer_start(m)

        for stage in stage_order(ex.stages)[:-1] if ex.stages else []:
            advance(stage)

        @pl.when((turn > 0) & (m < chunks))
        def _():
            layer_rest(turn - 1, m)

    @pl.loop(0, chunks)
    def _(m):
        store(m).wait()

    @pl.loop(0, chunks - kept)
    def _(i):
        keep_mixed(i).wait()

    keep_a().wait()


def body(state_field, spectral_x, spectral_y, expand_weight, reduce_weight):
    planes, channels, rows, cols = state_field.shape
    layers, hidden = expand_weight.shape[0], expand_weight.shape[2]
    gx, gy = lax.axis_size("gx"), lax.axis_size("gy")
    nx, ny = rows * gx, cols * gy
    modes = spectral_x.shape[1] * gx
    rows2 = 2 * modes
    chunks = cols // LANES
    bf16, f32 = jnp.bfloat16, jnp.float32
    own_y = spectral_y.shape[1]
    own_x = spectral_x.shape[1]
    forward_x, inverse_x = local_tables(
        lax.axis_index("gx") * rows, rows, nx, mode_order(modes, gx)
    )
    forward_y, inverse_y = local_tables(
        lax.axis_index("gy") * cols, cols, ny, mode_order(modes, gy)
    )

    args = [
        state_field.reshape(channels, rows, cols),
        forward_x,
        forward_y,
        inverse_x,
        inverse_y,
        spectral_x,
        spectral_y,
        expand_weight,
        jnp.swapaxes(reduce_weight, 1, 2),
    ]
    bits_x, bits_y = gx.bit_length() - 1, gy.bit_length() - 1
    per_x, per_y = rows2 // gx, rows2 // gy
    early, gap = pl.cdiv(chunks, 2), 2
    period = max(chunks, 2 * bits_x, early + 4 * bits_y - 1)
    kept = max(0, chunks - 2, chunks + 2 * bits_x - period - gap)
    tail = chunks - kept
    m_rows = max(channels, rows2) * (max(channels, rows2) + PAD)
    scratch = [
        pltpu.VMEM((chunks, channels, rows, LANES), bf16),
        pltpu.VMEM((chunks, gx, per_x, channels, LANES), bf16),
        pltpu.VMEM((chunks, gx, per_x, channels, LANES), bf16),
        pltpu.VMEM((1, gy, per_y, channels, rows), bf16),
        pltpu.VMEM((1, gy, per_y, channels, rows), bf16),
        pltpu.VMEM((channels * (rows + PAD), LANES), f32),
        pltpu.VMEM((channels * (rows + PAD), LANES), f32),
        pltpu.VMEM((hidden, GROUP * LANES), bf16),
        pltpu.VMEM((hidden, GROUP * LANES), bf16),
        pltpu.VMEM((m_rows, LANES), f32),
        pltpu.VMEM((m_rows, rows), f32),
        pltpu.VMEM((channels, rows, 2 * rows2), bf16),
        pltpu.VMEM((layers, own_x, 2 * channels, 2 * channels), bf16),
        pltpu.VMEM((layers, own_y, 2 * channels, 2 * channels), bf16),
        pltpu.VMEM((layers, hidden, channels), bf16),
        pltpu.VMEM((layers, channels, hidden), bf16),
    ]
    for s in range(bits_x):
        scratch.append(pltpu.VMEM((chunks, gx >> (s + 1), per_x, channels, LANES), bf16))
    for s in range(bits_y):
        scratch.append(pltpu.VMEM((1, gy >> (s + 1), per_y, channels, rows), bf16))
    dma = pltpu.SemaphoreType.DMA
    scratch += [dma((2 * bits_x, chunks))] * 2 + [dma((2 * bits_y, 1))] * 2 + [dma((chunks,))] * 2
    scratch += [dma((chunks - kept,)), dma(())]
    vmem = pl.BlockSpec(memory_space=pltpu.VMEM)
    anywhere = pl.BlockSpec(memory_space=pl.ANY)
    state_shape = jax.ShapeDtypeStruct((channels, rows, cols), bf16)
    mixed_shape = jax.ShapeDtypeStruct((tail, gx, per_x, channels, LANES), bf16)
    a_shape = jax.ShapeDtypeStruct((channels, rows, 2 * rows2), bf16)
    state, mixed, a = pl.pallas_call(
        functools.partial(mega, layers, gx, gy, (early, period, gap, kept)),
        name="layers",
        out_shape=[state_shape, mixed_shape, a_shape],
        in_specs=[anywhere] + [vmem] * (len(args) - 1),
        out_specs=[anywhere] * 3,
        scratch_shapes=scratch,
        compiler_params=pltpu.CompilerParams(
            collective_id=0, has_side_effects=True, vmem_limit_bytes=67043328
        ),
    )(*args)
    out = pl.pallas_call(
        functools.partial(tail_kernel, kept),
        name="tail",
        out_shape=state_shape,
        in_specs=[anywhere] * 3 + [vmem] * 3,
        out_specs=anywhere,
        scratch_shapes=[
            pltpu.VMEM((chunks, channels, rows, LANES), bf16),
            pltpu.VMEM(mixed_shape.shape, bf16),
            pltpu.VMEM(a_shape.shape, bf16),
            pltpu.VMEM((channels * (rows + PAD), LANES), f32),
            pltpu.VMEM((channels * (rows + PAD), LANES), f32),
            pltpu.VMEM((hidden, GROUP * LANES), bf16),
            pltpu.VMEM((hidden, GROUP * LANES), bf16),
            pltpu.VMEM((m_rows, LANES), f32),
            dma((chunks,)),
            dma((tail,)),
            dma(()),
            dma((chunks,)),
        ],
        compiler_params=pltpu.CompilerParams(vmem_limit_bytes=60 * 1024 * 1024),
    )(state, mixed, a, inverse_y, expand_weight[-1], args[-1][-1])
    return out.reshape(state_field.shape)


def solution(mesh):
    in_specs = (
        P(None, None, "gx", "gy"),
        P(None, "gx", None, None, None),
        P(None, "gy", None, None, None),
        P(),
        P(),
    )
    out_specs = P(None, None, "gx", "gy")
    return jax.shard_map(body, mesh=mesh, in_specs=in_specs, out_specs=out_specs, check_vma=False)
```

```python
import functools

import jax
import jax.numpy as jnp
from jax import lax
from jax.experimental import pallas as pl
from jax.experimental.pallas import tpu as pltpu
from jax.sharding import PartitionSpec as P

LANES = 128
PAD = 4
GROUP = 8
FIRST = 3
WIDE = 16
GELU_A = 0.7978845608028654
GELU_B = 0.044715
GELU_S = (GELU_A * GELU_B) ** (1.0 / 3.0)
MESH = pl.DeviceIdType.MESH


def bit_reversed(count):
    bits = count.bit_length() - 1
    return [int(format(i, "b").zfill(bits)[::-1], 2) if bits else 0 for i in range(count)]


def mode_order(modes, owners):
    each = modes // owners
    return [o * each + j for o in bit_reversed(owners) for j in range(each)]


def local_tables(first, count, length, order):
    rows2 = 2 * len(order)
    positions = first + jnp.arange(count, dtype=jnp.int32)
    orders = jnp.array([k for k in order for _ in range(2)], dtype=jnp.int32)[:, None]
    part = lax.broadcasted_iota(jnp.int32, (rows2, count), 0) % 2
    steps = (4 * orders * positions[None, :] + part * length) % (4 * length)
    factor = 1.0 / jnp.sqrt(jnp.float32(length))
    forward = jnp.cos(jnp.pi * steps.astype(jnp.float32) / (2 * length)) * factor
    inverse = jnp.where(orders == 0, 1.0, 2.0) * forward
    return forward.astype(jnp.bfloat16), inverse.astype(jnp.bfloat16)


def dot(left, right):
    return jnp.dot(left, right, preferred_element_type=jnp.float32)


def dot_nt(left, right):
    return lax.dot_general(
        left, right, (((1,), (1,)), ((), ())), preferred_element_type=jnp.float32
    )


def stage_ends(stages):
    spans = [2 if stages >= 4 and s in (1, stages - 2) else 1 for s in range(stages)]
    return [sum(spans[: s + 1]) for s in range(stages)]


def stage_order(stages):
    if stages < 4:
        return list(reversed(range(stages)))
    first, late = [stages - 1, stages - 3, 0], [stages - 2, 1]
    middle = [s for s in reversed(range(stages)) if s not in first + late]
    return list(dict.fromkeys(first + middle + late))


def schedule(chunks, stages, y_stages):
    late = (stage_ends(stages)[-1] + 1) // 2 if stages else 0
    early = pl.cdiv(chunks, FIRST)
    first = max(late, early + max(y_stages - 1, 0), 1)
    base = max(chunks, first + 1)
    second = max(first + chunks + y_stages, base + late)
    kept = min(chunks, max(0, chunks - 2, base + chunks + late - second))
    return first, second - first, base, kept


class Exchange:
    def __init__(self, axis, size, send, full, recv, send_sem, recv_sem, mix):
        self.axis, self.size = axis, size
        self.bits = size.bit_length() - 1
        self.stages = 2 * self.bits
        self.send, self.full, self.recv = send, full, recv
        self.send_sem, self.recv_sem = send_sem, recv_sem
        self.mix = mix
        self.me = lax.axis_index(axis)

    def bit(self, s):
        return lax.rem(self.me // (1 << s), 2)

    def base(self, s):
        total = 0
        for b in range(s):
            total = total + self.bit(b) * (self.size >> (b + 1))
        return total

    def partner(self, s):
        return self.me + (1 - 2 * self.bit(s)) * (1 << s)

    def copy(self, stage, m):
        if stage < self.bits:
            half = self.size >> (stage + 1)
            start = self.base(stage) + (1 - self.bit(stage)) * half
            src = self.send.at[m, pl.ds(start, half)]
            dst = self.recv[stage].at[m]
            peer = self.partner(stage)
        else:
            s = self.stages - 1 - stage
            half = self.size >> (s + 1)
            src = self.full.at[m, pl.ds(self.base(s + 1), half)]
            dst = self.full.at[m, pl.ds(self.base(s + 1), half)]
            peer = self.partner(s)
        return pltpu.make_async_remote_copy(
            src_ref=src,
            dst_ref=dst,
            send_sem=self.send_sem.at[stage, m],
            recv_sem=self.recv_sem.at[stage, m],
            device_id={self.axis: peer},
            device_id_type=MESH,
        )

    def start(self, stage, m):
        self.copy(stage, m).start()

    def finish(self, stage, layer, m):
        self.copy(stage, m).wait()
        if stage < self.bits:
            half = self.size >> (stage + 1)
            keep = self.base(stage + 1)
            rows = self.send.shape[2]
            got = self.recv[stage]

            @pl.loop(0, half)
            def _(i):
                for r in range(rows):
                    self.send[m, keep + i, r] = self.send[m, keep + i, r] + got[m, i, r]

            if stage == self.bits - 1:
                self.mix(layer, m, self.base(self.bits))
        if stage + 1 < self.stages:
            self.start(stage + 1, m)


def transform(mixed_ref, a_ref, iy, m_ref, t_ref):
    owners, each, channels, _ = mixed_ref.shape
    rows, rows2 = a_ref.shape[1], owners * each
    t_step, m_step = rows + PAD, channels + PAD
    for p in range(owners):
        for r in range(each):
            at = pl.ds((p * each + r) * m_step, channels)
            m_ref[at, :] = mixed_ref[p, r].astype(jnp.float32)

    @pl.loop(0, channels // WIDE)
    def _(g):
        for i in range(WIDE):
            c = g * WIDE + i
            part = m_ref[pl.ds(c, rows2, stride=m_step), :].astype(jnp.bfloat16)
            t_ref[pl.ds(c * t_step, rows), :] = dot(a_ref[c], jnp.concatenate([part, iy], axis=0))


def pointwise(w1, w2, rows, t_ref, u_ref, h0_ref, h1_ref, begin=True, end=True):
    steps = rows // (2 * GROUP)
    low, high = (0 if begin else steps // 2), (steps if end else steps // 2)
    channels, t_step = w2.shape[0], rows + PAD
    cg = jnp.bfloat16(GELU_A / GELU_S)

    def expand(base, h_ref):
        parts = [t_ref[pl.ds(base + i, channels, stride=t_step), :] for i in range(GROUP)]
        wide = jnp.concatenate(parts, axis=1).astype(jnp.bfloat16)
        h_ref[...] = dot(w1, wide).astype(jnp.bfloat16)

    def reduce(base, h_ref):
        h = h_ref[...]
        u = dot(w2, h + h * jnp.tanh(h * (h * h + cg)))
        for i in range(GROUP):
            u_ref[pl.ds(base + i, channels, stride=t_step), :] = u[:, i * LANES : (i + 1) * LANES]

    if begin:
        expand(0, h0_ref)

    @pl.loop(low, high)
    def _(g):
        base = g * 2 * GROUP
        expand(base + GROUP, h1_ref)
        reduce(base, h0_ref)
        expand(lax.rem(base + 2 * GROUP, rows), h0_ref)
        reduce(base + GROUP, h1_ref)


def add_update(st_ref, u_ref, c):
    rows = st_ref.shape[1]
    new = st_ref[c].astype(jnp.float32) + u_ref[pl.ds(c * (rows + PAD), rows), :]
    new = new.astype(jnp.bfloat16)
    st_ref[c] = new
    return new


def add_updates(st_ref, u_ref):
    @pl.loop(0, st_ref.shape[0] // 4)
    def _(g):
        for i in range(4):
            add_update(st_ref, u_ref, g * 4 + i)


def scaled_weights(ew, rw):
    w1 = (ew.astype(jnp.float32) * GELU_S).T.astype(jnp.bfloat16)
    return w1, (rw.astype(jnp.float32) * (0.5 / GELU_S)).astype(jnp.bfloat16)


def lanes(m):
    return pl.ds(pl.multiple_of(m * LANES, LANES), LANES)


def tail_kernel(kept, x_ref, mixed_ref, a_hbm, iy_ref, ew_ref, rw_ref, out_ref, *scratch):
    st, mx, a_ref, t_ref, u_ref, h0_ref, h1_ref, m_ref = scratch[:8]
    load_sem, mixed_sem, a_sem, store_sem = scratch[8:]
    chunks, _, rows, _ = st.shape

    def load(m):
        return pltpu.make_async_copy(x_ref.at[:, :, lanes(m)], st.at[m], load_sem.at[m])

    def store(m):
        return pltpu.make_async_copy(st.at[m], out_ref.at[:, :, lanes(m)], store_sem.at[m])

    def mixed(i):
        return pltpu.make_async_copy(mixed_ref.at[i], mx.at[i], mixed_sem.at[i])

    whole_a = pltpu.make_async_copy(a_hbm, a_ref, a_sem)
    whole_a.start()
    for i in range(chunks - kept):
        mixed(i).start()
        load(kept + i).start()
    for m in range(kept):
        load(m).start()
    w1, w2 = scaled_weights(ew_ref[ew_ref.shape[0] - 1], rw_ref[rw_ref.shape[0] - 1])
    whole_a.wait()

    @pl.loop(kept, chunks)
    def _(m):
        mixed(m - kept).wait()
        transform(mx.at[m - kept], a_ref, iy_ref[:, lanes(m)], m_ref, t_ref)
        pointwise(w1, w2, rows, t_ref, u_ref, h0_ref, h1_ref)
        load(m).wait()
        add_updates(st.at[m], u_ref)
        store(m).start()

        @pl.when(m == kept)
        def _():
            for other in range(kept):
                load(other).wait()
                store(other).start()

    @pl.loop(0, chunks)
    def _(m):
        store(m).wait()


def mega(layers, gx, gy, plan, state_ref, fx_ref, fy_ref, ixt_ref, iy_ref, spx_ref, spy_ref,
         ew_ref, rw_ref, out_ref, mixed_out, a_out, *scratch):
    first, later, base, kept = plan
    scratch = list(scratch)
    st, sx, mx, sy, my, t_ref, u_ref, h0_ref, h1_ref, m_ref, acc_ref, a_ref = scratch[:12]
    matx_ref, maty_ref, w1_ref, w2_ref = scratch[12:16]
    bits_x, bits_y = gx.bit_length() - 1, gy.bit_length() - 1
    rx = scratch[16 : 16 + bits_x]
    ry = scratch[16 + bits_x : 16 + bits_x + bits_y]
    sendx, recvx, sendy, recvy, load_sem, store_sem, mixed_sem, a_sem = scratch[16 + bits_x + bits_y :]
    chunks, channels, rows, _ = st.shape
    rows2 = fx_ref.shape[0]
    per_x, per_y = rows2 // gx, rows2 // gy
    t_step, m_step = rows + PAD, channels + PAD
    bf16, f32 = jnp.bfloat16, jnp.float32

    def mix_x(layer, m, at):
        for j in range(per_x // 2):
            pair = sx[m, at, 2 * j : 2 * j + 2].reshape(2 * channels, LANES)
            got = dot(matx_ref[layer, j], pair).astype(bf16)
            mx[m, at, 2 * j : 2 * j + 2] = got.reshape(2, channels, LANES)

    def mix_y(layer, m, at):
        @pl.loop(0, per_y // 2)
        def _(j):
            pair = sy[m, at, pl.ds(2 * j, 2)].reshape(2 * channels, rows)
            got = dot(maty_ref[layer, j], pair).astype(bf16)
            my[m, at, pl.ds(2 * j, 2)] = got.reshape(2, channels, rows)

    ex = Exchange("gx", gx, sx, mx, rx, sendx, recvx, mix_x)
    ey = Exchange("gy", gy, sy, my, ry, sendy, recvy, mix_y)

    def prepare():
        for layer in range(layers):
            w1_ref[layer], w2_ref[layer] = scaled_weights(ew_ref[layer], rw_ref[layer])
            for source, target in ((spx_ref, matx_ref), (spy_ref, maty_ref)):

                @pl.loop(0, source.shape[1])
                def _(j):
                    real, imag = source[layer, j, 0], source[layer, j, 1]
                    target[layer, j, :channels] = jnp.concatenate([real, -imag], axis=1)
                    target[layer, j, channels:] = jnp.concatenate([imag, real], axis=1)

    def load(m):
        return pltpu.make_async_copy(state_ref.at[:, :, lanes(m)], st.at[m], load_sem.at[m])

    def store(m):
        return pltpu.make_async_copy(st.at[m], out_ref.at[:, :, lanes(m)], store_sem.at[m])

    def keep_mixed(i):
        return pltpu.make_async_copy(mx.at[kept + i], mixed_out.at[i], mixed_sem.at[i])

    def keep_a():
        return pltpu.make_async_copy(a_ref, a_out, a_sem)

    def spectra(base, news, fx, fy):
        count = len(news)
        wide = dot(fx, jnp.concatenate(news, axis=1))
        tall = dot_nt(fy, jnp.concatenate(news, axis=0))
        for i in range(count):
            at = pl.ds((base + i) * m_step, rows2)
            m_ref[at, :] = wide[:, i * LANES : (i + 1) * LANES]
            acc_ref[at, :] = acc_ref[at, :] + tall[:, i * rows : (i + 1) * rows]

    def clear(m):
        @pl.when(m == 0)
        def _():
            acc_ref[...] = jnp.zeros_like(acc_ref)

    def send_spectra(m):
        for p in range(gx):
            for r in range(per_x):
                k = p * per_x + r
                sx[m, p, r] = m_ref[pl.ds(k, channels, stride=m_step), :].astype(bf16)
        ex.start(0, m)

        @pl.when(m == chunks - 1)
        def _():
            for p in range(gy):
                for r in range(per_y):
                    k = p * per_y + r
                    sy[0, p, r] = acc_ref[pl.ds(k, channels, stride=m_step), :].astype(bf16)
            if bits_y:
                ey.start(0, 0)

    def first_task(m):
        load(m).wait()
        clear(m)
        fx, fy = fx_ref[...], fy_ref[:, lanes(m)]

        @pl.loop(0, channels // WIDE)
        def _(g):
            base = g * WIDE
            spectra(base, [st[m, base + i] for i in range(WIDE)], fx, fy)

        send_spectra(m)

    def build_a():
        for p in range(gy):
            for r in range(per_y):
                at = pl.ds((p * per_y + r) * m_step, channels)
                acc_ref[at, :] = my[0, p, r].astype(f32)
        top = ixt_ref[...].astype(f32)

        @pl.loop(0, channels // 8)
        def _(g):
            for i in range(8):
                low = acc_ref[pl.ds(g * 8 + i, rows2, stride=m_step), :]
                a_ref[g * 8 + i] = jnp.concatenate([top, low], axis=0).T.astype(bf16)

    def layer_start(layer, m):
        transform(mx.at[m], a_ref, iy_ref[:, lanes(m)], m_ref, t_ref)
        network(layer, end=False)

    def network(layer, **part):
        pointwise(w1_ref[layer], w2_ref[layer], rows, t_ref, u_ref, h0_ref, h1_ref, **part)

    def layer_rest(layer, m):
        network(layer, begin=False)

        @pl.when(layer < layers - 1)
        def _():
            clear(m)
            fx, fy = fx_ref[...], fy_ref[:, lanes(m)]

            @pl.loop(0, channels // WIDE)
            def _(g):
                base = g * WIDE
                spectra(base, [add_update(st.at[m], u_ref, base + i) for i in range(WIDE)], fx, fy)

            send_spectra(m)

        @pl.when((layer == layers - 2) & (m >= kept))
        def _():
            store(m).start()

        @pl.when(layer == layers - 1)
        def _():
            add_updates(st.at[m], u_ref)
            store(m).start()

    barrier = pltpu.get_barrier_semaphore()
    for one in (ex, ey):
        for s in range(one.bits):
            pl.semaphore_signal(
                barrier, inc=1, device_id={one.axis: one.partner(s)}, device_id_type=MESH
            )

    @pl.loop(0, chunks)
    def _(m):
        load(m).start()

    pl.semaphore_wait(barrier, ex.bits + ey.bits)

    prepare()
    ends = stage_ends(ex.stages)

    def place(t, start):
        after = jnp.maximum(t - start, 0)
        turn = jnp.where(t < start, 0, 1 + after // later)
        return turn, jnp.where(t < start, t, lax.rem(after, later))

    @pl.loop(0, first + (layers - 1) * later + kept)
    def _(t):
        turn, m = place(t, first)

        def advance(half):
            for stage in stage_order(ex.stages):
                if ends[stage] % 2 == half:
                    ago = ends[stage] // 2
                    layer, chunk = place(t - ago, base)

                    @pl.when((t >= ago) & (chunk < chunks) & (layer < layers))
                    def _():
                        ex.finish(stage, layer, chunk)
                        if stage == ex.stages - 1:

                            @pl.when((layer == layers - 1) & (chunk >= kept))
                            def _():
                                keep_mixed(chunk - kept).start()

        advance(0)
        for stage in range(ey.stages):
            since = t - first + ey.stages - 1 - stage

            @pl.when((since >= 0) & (lax.rem(jnp.maximum(since, 0), later) == 0))
            def _():
                ey.finish(stage, jnp.maximum(since, 0) // later, 0)

        for i in range(FIRST):

            @pl.when(FIRST * t + i < chunks)
            def _():
                first_task(FIRST * t + i)

        @pl.when((turn > 0) & (m == 0))
        def _():
            build_a()

            @pl.when(turn == layers)
            def _():
                keep_a().start()

        @pl.when((turn > 0) & (m < chunks))
        def _():
            layer_start(turn - 1, m)

        advance(1)

        @pl.when((turn > 0) & (m < chunks))
        def _():
            layer_rest(turn - 1, m)

    @pl.loop(0, chunks)
    def _(m):
        store(m).wait()

    @pl.loop(0, chunks - kept)
    def _(i):
        keep_mixed(i).wait()

    keep_a().wait()


def body(state_field, spectral_x, spectral_y, expand_weight, reduce_weight):
    planes, channels, rows, cols = state_field.shape
    layers, hidden = expand_weight.shape[0], expand_weight.shape[2]
    gx, gy = lax.axis_size("gx"), lax.axis_size("gy")
    nx, ny = rows * gx, cols * gy
    modes = spectral_x.shape[1] * gx
    rows2 = 2 * modes
    chunks = cols // LANES
    bf16, f32 = jnp.bfloat16, jnp.float32
    own_y = spectral_y.shape[1]
    own_x = spectral_x.shape[1]
    forward_x, inverse_x = local_tables(
        lax.axis_index("gx") * rows, rows, nx, mode_order(modes, gx)
    )
    forward_y, inverse_y = local_tables(
        lax.axis_index("gy") * cols, cols, ny, mode_order(modes, gy)
    )

    args = [
        state_field.reshape(channels, rows, cols),
        forward_x,
        forward_y,
        inverse_x,
        inverse_y,
        spectral_x,
        spectral_y,
        expand_weight,
        jnp.swapaxes(reduce_weight, 1, 2),
    ]
    bits_x, bits_y = gx.bit_length() - 1, gy.bit_length() - 1
    per_x, per_y = rows2 // gx, rows2 // gy
    plan = schedule(chunks, 2 * bits_x, 2 * bits_y)
    kept = plan[-1]
    tail = chunks - kept
    m_rows = max(channels, rows2) * (max(channels, rows2) + PAD)
    scratch = [
        pltpu.VMEM((chunks, channels, rows, LANES), bf16),
        pltpu.VMEM((chunks, gx, per_x, channels, LANES), bf16),
        pltpu.VMEM((chunks, gx, per_x, channels, LANES), bf16),
        pltpu.VMEM((1, gy, per_y, channels, rows), bf16),
        pltpu.VMEM((1, gy, per_y, channels, rows), bf16),
        pltpu.VMEM((channels * (rows + PAD), LANES), f32),
        pltpu.VMEM((channels * (rows + PAD), LANES), f32),
        pltpu.VMEM((hidden, GROUP * LANES), bf16),
        pltpu.VMEM((hidden, GROUP * LANES), bf16),
        pltpu.VMEM((m_rows, LANES), f32),
        pltpu.VMEM((m_rows, rows), f32),
        pltpu.VMEM((channels, rows, 2 * rows2), bf16),
        pltpu.VMEM((layers, own_x, 2 * channels, 2 * channels), bf16),
        pltpu.VMEM((layers, own_y, 2 * channels, 2 * channels), bf16),
        pltpu.VMEM((layers, hidden, channels), bf16),
        pltpu.VMEM((layers, channels, hidden), bf16),
    ]
    for s in range(bits_x):
        scratch.append(pltpu.VMEM((chunks, gx >> (s + 1), per_x, channels, LANES), bf16))
    for s in range(bits_y):
        scratch.append(pltpu.VMEM((1, gy >> (s + 1), per_y, channels, rows), bf16))
    dma = pltpu.SemaphoreType.DMA
    scratch += [dma((2 * bits_x, chunks))] * 2 + [dma((2 * bits_y, 1))] * 2 + [dma((chunks,))] * 2
    scratch += [dma((chunks - kept,)), dma(())]
    vmem = pl.BlockSpec(memory_space=pltpu.VMEM)
    anywhere = pl.BlockSpec(memory_space=pl.ANY)
    state_shape = jax.ShapeDtypeStruct((channels, rows, cols), bf16)
    mixed_shape = jax.ShapeDtypeStruct((tail, gx, per_x, channels, LANES), bf16)
    a_shape = jax.ShapeDtypeStruct((channels, rows, 2 * rows2), bf16)
    state, mixed, a = pl.pallas_call(
        functools.partial(mega, layers, gx, gy, plan),
        name="layers",
        out_shape=[state_shape, mixed_shape, a_shape],
        in_specs=[anywhere] + [vmem] * (len(args) - 1),
        out_specs=[anywhere] * 3,
        scratch_shapes=scratch,
        compiler_params=pltpu.CompilerParams(
            collective_id=0, has_side_effects=True, vmem_limit_bytes=67043328
        ),
    )(*args)
    out = pl.pallas_call(
        functools.partial(tail_kernel, kept),
        name="tail",
        out_shape=state_shape,
        in_specs=[anywhere] * 3 + [vmem] * 3,
        out_specs=anywhere,
        scratch_shapes=[
            pltpu.VMEM((chunks, channels, rows, LANES), bf16),
            pltpu.VMEM(mixed_shape.shape, bf16),
            pltpu.VMEM(a_shape.shape, bf16),
            pltpu.VMEM((channels * (rows + PAD), LANES), f32),
            pltpu.VMEM((channels * (rows + PAD), LANES), f32),
            pltpu.VMEM((hidden, GROUP * LANES), bf16),
            pltpu.VMEM((hidden, GROUP * LANES), bf16),
            pltpu.VMEM((m_rows, LANES), f32),
            dma((chunks,)),
            dma((tail,)),
            dma(()),
            dma((chunks,)),
        ],
        compiler_params=pltpu.CompilerParams(vmem_limit_bytes=60 * 1024 * 1024),
    )(state, mixed, a, inverse_y, *args[-2:])
    return out.reshape(state_field.shape)


def solution(mesh):
    in_specs = (
        P(None, None, "gx", "gy"),
        P(None, "gx", None, None, None),
        P(None, "gy", None, None, None),
        P(),
        P(),
    )
    out_specs = P(None, None, "gx", "gy")
    return jax.shard_map(body, mesh=mesh, in_specs=in_specs, out_specs=out_specs, check_vma=False)
```

```python
import functools

import jax
import jax.numpy as jnp
from jax import lax
from jax.experimental import pallas as pl
from jax.experimental.pallas import tpu as pltpu
from jax.sharding import PartitionSpec as P

LANES = 128
PAD = 4
GROUP = 8
FIRST = 3
WIDE = 16
GELU_A = 0.7978845608028654
GELU_B = 0.044715
GELU_S = (GELU_A * GELU_B) ** (1.0 / 3.0)
MESH = pl.DeviceIdType.MESH


def bit_reversed(count):
    bits = count.bit_length() - 1
    return [int(format(i, "b").zfill(bits)[::-1], 2) if bits else 0 for i in range(count)]


def mode_order(modes, owners):
    each = modes // owners
    return [o * each + j for o in bit_reversed(owners) for j in range(each)]


def local_tables(first, count, length, order):
    rows2 = 2 * len(order)
    positions = first + jnp.arange(count, dtype=jnp.int32)
    orders = jnp.array([k for k in order for _ in range(2)], dtype=jnp.int32)[:, None]
    part = lax.broadcasted_iota(jnp.int32, (rows2, count), 0) % 2
    steps = (4 * orders * positions[None, :] + part * length) % (4 * length)
    factor = 1.0 / jnp.sqrt(jnp.float32(length))
    forward = jnp.cos(jnp.pi * steps.astype(jnp.float32) / (2 * length)) * factor
    inverse = jnp.where(orders == 0, 1.0, 2.0) * forward
    return forward.astype(jnp.bfloat16), inverse.astype(jnp.bfloat16)


def dot(left, right):
    return jnp.dot(left, right, preferred_element_type=jnp.float32)


def dot_nt(left, right):
    return lax.dot_general(
        left, right, (((1,), (1,)), ((), ())), preferred_element_type=jnp.float32
    )


def stage_ends(stages):
    spans = [2 if stages >= 4 and s in (1, stages // 2 - 1, stages // 2, stages - 2) else 1 for s in range(stages)]
    return [sum(spans[: s + 1]) for s in range(stages)]


def stage_order(stages):
    if stages < 4:
        return list(reversed(range(stages)))
    first, late = [stages - 1, stages - 3, 0], [stages - 2, 1]
    middle = [s for s in reversed(range(stages)) if s not in first + late]
    return list(dict.fromkeys(first + middle + late))


def schedule(chunks, stages, y_stages):
    late = (stage_ends(stages)[-1] + 1) // 2 if stages else 0
    early = pl.cdiv(chunks, FIRST)
    first = max(late, early + max(y_stages - 1, 0), 1)
    base = max(chunks, first + 1)
    second = max(first + chunks + y_stages, base + late + 1)
    kept = min(chunks, max(0, chunks - 2, base + chunks + late - second))
    return first, second - first, base, kept


class Exchange:
    def __init__(self, axis, size, send, full, recv, send_sem, recv_sem, mix):
        self.axis, self.size = axis, size
        self.bits = size.bit_length() - 1
        self.stages = 2 * self.bits
        self.send, self.full, self.recv = send, full, recv
        self.send_sem, self.recv_sem = send_sem, recv_sem
        self.mix = mix
        self.me = lax.axis_index(axis)

    def bit(self, s):
        return lax.rem(self.me // (1 << s), 2)

    def base(self, s):
        total = 0
        for b in range(s):
            total = total + self.bit(b) * (self.size >> (b + 1))
        return total

    def partner(self, s):
        return self.me + (1 - 2 * self.bit(s)) * (1 << s)

    def copy(self, stage, m):
        if stage < self.bits:
            half = self.size >> (stage + 1)
            start = self.base(stage) + (1 - self.bit(stage)) * half
            src = self.send.at[m, pl.ds(start, half)]
            dst = self.recv[stage].at[m]
            peer = self.partner(stage)
        else:
            s = self.stages - 1 - stage
            half = self.size >> (s + 1)
            src = self.full.at[m, pl.ds(self.base(s + 1), half)]
            dst = self.full.at[m, pl.ds(self.base(s + 1), half)]
            peer = self.partner(s)
        return pltpu.make_async_remote_copy(
            src_ref=src,
            dst_ref=dst,
            send_sem=self.send_sem.at[stage, m],
            recv_sem=self.recv_sem.at[stage, m],
            device_id={self.axis: peer},
            device_id_type=MESH,
        )

    def start(self, stage, m):
        self.copy(stage, m).start()

    def finish(self, stage, layer, m):
        self.copy(stage, m).wait()
        if stage < self.bits:
            half = self.size >> (stage + 1)
            keep = self.base(stage + 1)
            rows = self.send.shape[2]
            got = self.recv[stage]

            @pl.loop(0, half)
            def _(i):
                for r in range(rows):
                    self.send[m, keep + i, r] = self.send[m, keep + i, r] + got[m, i, r]

            if stage == self.bits - 1:
                self.mix(layer, m, self.base(self.bits))
        if stage + 1 < self.stages:
            self.start(stage + 1, m)


def transform(mixed_ref, a_ref, iy, m_ref, t_ref):
    owners, each, channels, _ = mixed_ref.shape
    rows, rows2 = a_ref.shape[1], owners * each
    t_step, m_step = rows + PAD, channels + PAD
    for p in range(owners):
        for r in range(each):
            at = pl.ds((p * each + r) * m_step, channels)
            m_ref[at, :] = mixed_ref[p, r].astype(jnp.float32)

    @pl.loop(0, channels // WIDE)
    def _(g):
        for i in range(WIDE):
            c = g * WIDE + i
            part = m_ref[pl.ds(c, rows2, stride=m_step), :].astype(jnp.bfloat16)
            t_ref[pl.ds(c * t_step, rows), :] = dot(a_ref[c], jnp.concatenate([part, iy], axis=0))


def pointwise(w1, w2, rows, t_ref, u_ref, h0_ref, h1_ref, begin=True, end=True):
    steps = rows // (2 * GROUP)
    low, high = (0 if begin else steps // 2), (steps if end else steps // 2)
    channels, t_step = w2.shape[0], rows + PAD
    cg = jnp.bfloat16(GELU_A / GELU_S)

    def expand(base, h_ref):
        parts = [t_ref[pl.ds(base + i, channels, stride=t_step), :] for i in range(GROUP)]
        wide = jnp.concatenate(parts, axis=1).astype(jnp.bfloat16)
        h_ref[...] = dot(w1, wide).astype(jnp.bfloat16)

    def reduce(base, h_ref):
        h = h_ref[...]
        u = dot(w2, h + h * jnp.tanh(h * (h * h + cg)))
        for i in range(GROUP):
            u_ref[pl.ds(base + i, channels, stride=t_step), :] = u[:, i * LANES : (i + 1) * LANES]

    if begin:
        expand(0, h0_ref)

    @pl.loop(low, high)
    def _(g):
        base = g * 2 * GROUP
        expand(base + GROUP, h1_ref)
        reduce(base, h0_ref)
        expand(lax.rem(base + 2 * GROUP, rows), h0_ref)
        reduce(base + GROUP, h1_ref)


def add_update(st_ref, u_ref, c):
    rows = st_ref.shape[1]
    new = st_ref[c].astype(jnp.float32) + u_ref[pl.ds(c * (rows + PAD), rows), :]
    new = new.astype(jnp.bfloat16)
    st_ref[c] = new
    return new


def add_updates(st_ref, u_ref):
    @pl.loop(0, st_ref.shape[0] // 4)
    def _(g):
        for i in range(4):
            add_update(st_ref, u_ref, g * 4 + i)


def scaled_weights(ew, rw):
    w1 = (ew.astype(jnp.float32) * GELU_S).T.astype(jnp.bfloat16)
    return w1, (rw.astype(jnp.float32) * (0.5 / GELU_S)).astype(jnp.bfloat16)


def lanes(m):
    return pl.ds(pl.multiple_of(m * LANES, LANES), LANES)


def tail_kernel(kept, x_ref, mixed_ref, a_hbm, iy_ref, ew_ref, rw_ref, out_ref, *scratch):
    st, mx, a_ref, t_ref, u_ref, h0_ref, h1_ref, m_ref = scratch[:8]
    load_sem, mixed_sem, a_sem, store_sem = scratch[8:]
    chunks, _, rows, _ = st.shape

    def load(m):
        return pltpu.make_async_copy(x_ref.at[:, :, lanes(m)], st.at[m], load_sem.at[m])

    def store(m):
        return pltpu.make_async_copy(st.at[m], out_ref.at[:, :, lanes(m)], store_sem.at[m])

    def mixed(i):
        return pltpu.make_async_copy(mixed_ref.at[i], mx.at[i], mixed_sem.at[i])

    whole_a = pltpu.make_async_copy(a_hbm, a_ref, a_sem)
    whole_a.start()
    for i in range(chunks - kept):
        mixed(i).start()
        load(kept + i).start()
    for m in range(kept):
        load(m).start()
    w1, w2 = scaled_weights(ew_ref[ew_ref.shape[0] - 1], rw_ref[rw_ref.shape[0] - 1])
    whole_a.wait()

    @pl.loop(kept, chunks)
    def _(m):
        mixed(m - kept).wait()
        transform(mx.at[m - kept], a_ref, iy_ref[:, lanes(m)], m_ref, t_ref)
        pointwise(w1, w2, rows, t_ref, u_ref, h0_ref, h1_ref)
        load(m).wait()
        add_updates(st.at[m], u_ref)
        store(m).start()

        @pl.when(m == kept)
        def _():
            for other in range(kept):
                load(other).wait()
                store(other).start()

    @pl.loop(0, chunks)
    def _(m):
        store(m).wait()


def mega(layers, gx, gy, plan, state_ref, fx_ref, fy_ref, ixt_ref, iy_ref, spx_ref, spy_ref,
         ew_ref, rw_ref, out_ref, mixed_out, a_out, *scratch):
    first, later, base, kept = plan
    scratch = list(scratch)
    st, sx, mx, sy, my, t_ref, u_ref, h0_ref, h1_ref, m_ref, acc_ref, a_ref = scratch[:12]
    matx_ref, maty_ref, w1_ref, w2_ref = scratch[12:16]
    bits_x, bits_y = gx.bit_length() - 1, gy.bit_length() - 1
    rx = scratch[16 : 16 + bits_x]
    ry = scratch[16 + bits_x : 16 + bits_x + bits_y]
    sendx, recvx, sendy, recvy, load_sem, store_sem, mixed_sem, a_sem = scratch[16 + bits_x + bits_y :]
    chunks, channels, rows, _ = st.shape
    rows2 = fx_ref.shape[0]
    per_x, per_y = rows2 // gx, rows2 // gy
    t_step, m_step = rows + PAD, channels + PAD
    bf16, f32 = jnp.bfloat16, jnp.float32

    def mix_x(layer, m, at):
        for j in range(per_x // 2):
            pair = sx[m, at, 2 * j : 2 * j + 2].reshape(2 * channels, LANES)
            got = dot(matx_ref[layer, j], pair).astype(bf16)
            mx[m, at, 2 * j : 2 * j + 2] = got.reshape(2, channels, LANES)

    def mix_y(layer, m, at):
        @pl.loop(0, per_y // 2)
        def _(j):
            pair = sy[m, at, pl.ds(2 * j, 2)].reshape(2 * channels, rows)
            got = dot(maty_ref[layer, j], pair).astype(bf16)
            my[m, at, pl.ds(2 * j, 2)] = got.reshape(2, channels, rows)

    ex = Exchange("gx", gx, sx, mx, rx, sendx, recvx, mix_x)
    ey = Exchange("gy", gy, sy, my, ry, sendy, recvy, mix_y)

    def prepare():
        for layer in range(layers):
            w1_ref[layer], w2_ref[layer] = scaled_weights(ew_ref[layer], rw_ref[layer])
            for source, target in ((spx_ref, matx_ref), (spy_ref, maty_ref)):

                @pl.loop(0, source.shape[1])
                def _(j):
                    real, imag = source[layer, j, 0], source[layer, j, 1]
                    target[layer, j, :channels] = jnp.concatenate([real, -imag], axis=1)
                    target[layer, j, channels:] = jnp.concatenate([imag, real], axis=1)

    def load(m):
        return pltpu.make_async_copy(state_ref.at[:, :, lanes(m)], st.at[m], load_sem.at[m])

    def store(m):
        return pltpu.make_async_copy(st.at[m], out_ref.at[:, :, lanes(m)], store_sem.at[m])

    def keep_mixed(i):
        return pltpu.make_async_copy(mx.at[kept + i], mixed_out.at[i], mixed_sem.at[i])

    def keep_a():
        return pltpu.make_async_copy(a_ref, a_out, a_sem)

    def spectra(base, news, fx, fy):
        count = len(news)
        wide = dot(fx, jnp.concatenate(news, axis=1))
        tall = dot_nt(fy, jnp.concatenate(news, axis=0))
        for i in range(count):
            at = pl.ds((base + i) * m_step, rows2)
            m_ref[at, :] = wide[:, i * LANES : (i + 1) * LANES]
            acc_ref[at, :] = acc_ref[at, :] + tall[:, i * rows : (i + 1) * rows]

    def clear(m):
        @pl.when(m == 0)
        def _():
            acc_ref[...] = jnp.zeros_like(acc_ref)

    def send_spectra(m):
        for p in range(gx):
            for r in range(per_x):
                k = p * per_x + r
                sx[m, p, r] = m_ref[pl.ds(k, channels, stride=m_step), :].astype(bf16)
        ex.start(0, m)

        @pl.when(m == chunks - 1)
        def _():
            for p in range(gy):
                for r in range(per_y):
                    k = p * per_y + r
                    sy[0, p, r] = acc_ref[pl.ds(k, channels, stride=m_step), :].astype(bf16)
            if bits_y:
                ey.start(0, 0)

    def first_task(m):
        load(m).wait()
        clear(m)
        fx, fy = fx_ref[...], fy_ref[:, lanes(m)]

        @pl.loop(0, channels // WIDE)
        def _(g):
            base = g * WIDE
            spectra(base, [st[m, base + i] for i in range(WIDE)], fx, fy)

        send_spectra(m)

    def build_a():
        for p in range(gy):
            for r in range(per_y):
                at = pl.ds((p * per_y + r) * m_step, channels)
                acc_ref[at, :] = my[0, p, r].astype(f32)
        top = ixt_ref[...].astype(f32)

        @pl.loop(0, channels // 8)
        def _(g):
            for i in range(8):
                low = acc_ref[pl.ds(g * 8 + i, rows2, stride=m_step), :]
                a_ref[g * 8 + i] = jnp.concatenate([top, low], axis=0).T.astype(bf16)

    def layer_start(layer, m):
        transform(mx.at[m], a_ref, iy_ref[:, lanes(m)], m_ref, t_ref)
        network(layer, end=False)

    def network(layer, **part):
        pointwise(w1_ref[layer], w2_ref[layer], rows, t_ref, u_ref, h0_ref, h1_ref, **part)

    def layer_rest(layer, m):
        network(layer, begin=False)

        @pl.when(layer < layers - 1)
        def _():
            clear(m)
            fx, fy = fx_ref[...], fy_ref[:, lanes(m)]

            @pl.loop(0, channels // WIDE)
            def _(g):
                base = g * WIDE
                spectra(base, [add_update(st.at[m], u_ref, base + i) for i in range(WIDE)], fx, fy)

            send_spectra(m)

        @pl.when((layer == layers - 2) & (m >= kept))
        def _():
            store(m).start()

        @pl.when(layer == layers - 1)
        def _():
            add_updates(st.at[m], u_ref)
            store(m).start()

    barrier = pltpu.get_barrier_semaphore()
    for one in (ex, ey):
        for s in range(one.bits):
            pl.semaphore_signal(
                barrier, inc=1, device_id={one.axis: one.partner(s)}, device_id_type=MESH
            )

    @pl.loop(0, chunks)
    def _(m):
        load(m).start()

    pl.semaphore_wait(barrier, ex.bits + ey.bits)

    ends = stage_ends(ex.stages)

    def place(t, start):
        after = jnp.maximum(t - start, 0)
        turn = jnp.where(t < start, 0, 1 + after // later)
        return turn, jnp.where(t < start, t, lax.rem(after, later))

    @pl.loop(0, first + (layers - 1) * later + kept)
    def _(t):
        turn, m = place(t, first)

        def advance(half):
            for stage in stage_order(ex.stages):
                if ends[stage] % 2 == half:
                    ago = ends[stage] // 2
                    layer, chunk = place(t - ago, base)

                    @pl.when((t >= ago) & (chunk < chunks) & (layer < layers))
                    def _():
                        ex.finish(stage, layer, chunk)
                        if stage == ex.stages - 1:

                            @pl.when((layer == layers - 1) & (chunk >= kept))
                            def _():
                                keep_mixed(chunk - kept).start()

        advance(0)
        for stage in range(ey.stages):
            since = t - first + ey.stages - 1 - stage

            @pl.when((since >= 0) & (lax.rem(jnp.maximum(since, 0), later) == 0))
            def _():
                ey.finish(stage, jnp.maximum(since, 0) // later, 0)

        for i in range(FIRST):

            @pl.when(FIRST * t + i < chunks)
            def _():
                first_task(FIRST * t + i)

        @pl.when((turn > 0) & (m == 0))
        def _():
            build_a()

            @pl.when(turn == layers)
            def _():
                keep_a().start()

        @pl.when((turn > 0) & (m < chunks))
        def _():
            layer_start(turn - 1, m)

        advance(1)

        @pl.when(t == 0)
        def _():
            prepare()

        @pl.when((turn > 0) & (m < chunks))
        def _():
            layer_rest(turn - 1, m)

    @pl.loop(0, chunks)
    def _(m):
        store(m).wait()

    @pl.loop(0, chunks - kept)
    def _(i):
        keep_mixed(i).wait()

    keep_a().wait()


def body(state_field, spectral_x, spectral_y, expand_weight, reduce_weight):
    planes, channels, rows, cols = state_field.shape
    layers, hidden = expand_weight.shape[0], expand_weight.shape[2]
    gx, gy = lax.axis_size("gx"), lax.axis_size("gy")
    nx, ny = rows * gx, cols * gy
    modes = spectral_x.shape[1] * gx
    rows2 = 2 * modes
    chunks = cols // LANES
    bf16, f32 = jnp.bfloat16, jnp.float32
    own_y = spectral_y.shape[1]
    own_x = spectral_x.shape[1]
    forward_x, inverse_x = local_tables(
        lax.axis_index("gx") * rows, rows, nx, mode_order(modes, gx)
    )
    forward_y, inverse_y = local_tables(
        lax.axis_index("gy") * cols, cols, ny, mode_order(modes, gy)
    )

    args = [
        state_field.reshape(channels, rows, cols),
        forward_x,
        forward_y,
        inverse_x,
        inverse_y,
        spectral_x,
        spectral_y,
        expand_weight,
        jnp.swapaxes(reduce_weight, 1, 2),
    ]
    bits_x, bits_y = gx.bit_length() - 1, gy.bit_length() - 1
    per_x, per_y = rows2 // gx, rows2 // gy
    plan = schedule(chunks, 2 * bits_x, 2 * bits_y)
    kept = plan[-1]
    tail = chunks - kept
    m_rows = max(channels, rows2) * (max(channels, rows2) + PAD)
    scratch = [
        pltpu.VMEM((chunks, channels, rows, LANES), bf16),
        pltpu.VMEM((chunks, gx, per_x, channels, LANES), bf16),
        pltpu.VMEM((chunks, gx, per_x, channels, LANES), bf16),
        pltpu.VMEM((1, gy, per_y, channels, rows), bf16),
        pltpu.VMEM((1, gy, per_y, channels, rows), bf16),
        pltpu.VMEM((channels * (rows + PAD), LANES), f32),
        pltpu.VMEM((channels * (rows + PAD), LANES), f32),
        pltpu.VMEM((hidden, GROUP * LANES), bf16),
        pltpu.VMEM((hidden, GROUP * LANES), bf16),
        pltpu.VMEM((m_rows, LANES), f32),
        pltpu.VMEM((m_rows, rows), f32),
        pltpu.VMEM((channels, rows, 2 * rows2), bf16),
        pltpu.VMEM((layers, own_x, 2 * channels, 2 * channels), bf16),
        pltpu.VMEM((layers, own_y, 2 * channels, 2 * channels), bf16),
        pltpu.VMEM((layers, hidden, channels), bf16),
        pltpu.VMEM((layers, channels, hidden), bf16),
    ]
    for s in range(bits_x):
        scratch.append(pltpu.VMEM((chunks, gx >> (s + 1), per_x, channels, LANES), bf16))
    for s in range(bits_y):
        scratch.append(pltpu.VMEM((1, gy >> (s + 1), per_y, channels, rows), bf16))
    dma = pltpu.SemaphoreType.DMA
    scratch += [dma((2 * bits_x, chunks))] * 2 + [dma((2 * bits_y, 1))] * 2 + [dma((chunks,))] * 2
    scratch += [dma((chunks - kept,)), dma(())]
    vmem = pl.BlockSpec(memory_space=pltpu.VMEM)
    anywhere = pl.BlockSpec(memory_space=pl.ANY)
    state_shape = jax.ShapeDtypeStruct((channels, rows, cols), bf16)
    mixed_shape = jax.ShapeDtypeStruct((tail, gx, per_x, channels, LANES), bf16)
    a_shape = jax.ShapeDtypeStruct((channels, rows, 2 * rows2), bf16)
    state, mixed, a = pl.pallas_call(
        functools.partial(mega, layers, gx, gy, plan),
        name="layers",
        out_shape=[state_shape, mixed_shape, a_shape],
        in_specs=[anywhere] + [vmem] * (len(args) - 1),
        out_specs=[anywhere] * 3,
        scratch_shapes=scratch,
        compiler_params=pltpu.CompilerParams(
            collective_id=0, has_side_effects=True, vmem_limit_bytes=67043328
        ),
    )(*args)
    out = pl.pallas_call(
        functools.partial(tail_kernel, kept),
        name="tail",
        out_shape=state_shape,
        in_specs=[anywhere] * 3 + [vmem] * 3,
        out_specs=anywhere,
        scratch_shapes=[
            pltpu.VMEM((chunks, channels, rows, LANES), bf16),
            pltpu.VMEM(mixed_shape.shape, bf16),
            pltpu.VMEM(a_shape.shape, bf16),
            pltpu.VMEM((channels * (rows + PAD), LANES), f32),
            pltpu.VMEM((channels * (rows + PAD), LANES), f32),
            pltpu.VMEM((hidden, GROUP * LANES), bf16),
            pltpu.VMEM((hidden, GROUP * LANES), bf16),
            pltpu.VMEM((m_rows, LANES), f32),
            dma((chunks,)),
            dma((tail,)),
            dma(()),
            dma((chunks,)),
        ],
        compiler_params=pltpu.CompilerParams(vmem_limit_bytes=60 * 1024 * 1024),
    )(state, mixed, a, inverse_y, *args[-2:])
    return out.reshape(state_field.shape)


def solution(mesh):
    in_specs = (
        P(None, None, "gx", "gy"),
        P(None, "gx", None, None, None),
        P(None, "gy", None, None, None),
        P(),
        P(),
    )
    out_specs = P(None, None, "gx", "gy")
    return jax.shard_map(body, mesh=mesh, in_specs=in_specs, out_specs=out_specs, check_vma=False)
```

```python
import functools

import jax
import jax.numpy as jnp
from jax import lax
from jax.experimental import pallas as pl
from jax.experimental.pallas import tpu as pltpu
from jax.sharding import PartitionSpec as P

LANES = 128
PAD = 4
GROUP = 8
FIRST = 2
WIDE = 16
GELU_A = 0.7978845608028654
GELU_B = 0.044715
GELU_S = (GELU_A * GELU_B) ** (1.0 / 3.0)
MESH = pl.DeviceIdType.MESH


def bit_reversed(count):
    bits = count.bit_length() - 1
    return [int(format(i, "b").zfill(bits)[::-1], 2) if bits else 0 for i in range(count)]


def mode_order(modes, owners):
    each = modes // owners
    return [o * each + j for o in bit_reversed(owners) for j in range(each)]


def local_tables(first, count, length, order):
    rows2 = 2 * len(order)
    positions = first + jnp.arange(count, dtype=jnp.int32)
    orders = jnp.array([k for k in order for _ in range(2)], dtype=jnp.int32)[:, None]
    part = lax.broadcasted_iota(jnp.int32, (rows2, count), 0) % 2
    steps = (4 * orders * positions[None, :] + part * length) % (4 * length)
    factor = 1.0 / jnp.sqrt(jnp.float32(length))
    forward = jnp.cos(jnp.pi * steps.astype(jnp.float32) / (2 * length)) * factor
    inverse = jnp.where(orders == 0, 1.0, 2.0) * forward
    return forward.astype(jnp.bfloat16), inverse.astype(jnp.bfloat16)


def dot(left, right):
    return jnp.dot(left, right, preferred_element_type=jnp.float32)


def dot_nt(left, right):
    return lax.dot_general(
        left, right, (((1,), (1,)), ((), ())), preferred_element_type=jnp.float32
    )


def stage_ends(stages):
    spans = [2 if stages >= 4 and s in (1, stages // 2 - 1, stages // 2, stages - 2) else 1 for s in range(stages)]
    return [sum(spans[: s + 1]) for s in range(stages)]


def stage_order(stages):
    if stages < 4:
        return list(reversed(range(stages)))
    first, late = [stages - 1, stages - 3, 0], [stages - 2, 1]
    middle = [s for s in reversed(range(stages)) if s not in first + late]
    return list(dict.fromkeys(first + middle + late))


def schedule(chunks, stages, y_stages):
    late = (stage_ends(stages)[-1] + 1) // 2 if stages else 0
    early = pl.cdiv(chunks, FIRST)
    first = max(late, early + max(y_stages - 1, 0), 1)
    base = max(chunks, first + 1)
    second = max(first + chunks + y_stages, base + late + 1)
    kept = min(chunks, max(0, chunks - 2, base + chunks + late - second))
    return first, second - first, base, kept


class Exchange:
    def __init__(self, axis, size, send, full, recv, send_sem, recv_sem, mix):
        self.axis, self.size = axis, size
        self.bits = size.bit_length() - 1
        self.stages = 2 * self.bits
        self.send, self.full, self.recv = send, full, recv
        self.send_sem, self.recv_sem = send_sem, recv_sem
        self.mix = mix
        self.me = lax.axis_index(axis)

    def bit(self, s):
        return lax.rem(self.me // (1 << s), 2)

    def base(self, s):
        total = 0
        for b in range(s):
            total = total + self.bit(b) * (self.size >> (b + 1))
        return total

    def partner(self, s):
        return self.me + (1 - 2 * self.bit(s)) * (1 << s)

    def copy(self, stage, m):
        if stage < self.bits:
            half = self.size >> (stage + 1)
            start = self.base(stage) + (1 - self.bit(stage)) * half
            src = self.send.at[m, pl.ds(start, half)]
            dst = self.recv[stage].at[m]
            peer = self.partner(stage)
        else:
            s = self.stages - 1 - stage
            half = self.size >> (s + 1)
            src = self.full.at[m, pl.ds(self.base(s + 1), half)]
            dst = self.full.at[m, pl.ds(self.base(s + 1), half)]
            peer = self.partner(s)
        return pltpu.make_async_remote_copy(
            src_ref=src,
            dst_ref=dst,
            send_sem=self.send_sem.at[stage, m],
            recv_sem=self.recv_sem.at[stage, m],
            device_id={self.axis: peer},
            device_id_type=MESH,
        )

    def start(self, stage, m):
        self.copy(stage, m).start()

    def finish(self, stage, layer, m):
        self.copy(stage, m).wait()
        if stage < self.bits:
            half = self.size >> (stage + 1)
            keep = self.base(stage + 1)
            rows = self.send.shape[2]
            got = self.recv[stage]

            @pl.loop(0, half)
            def _(i):
                for r in range(rows):
                    self.send[m, keep + i, r] = self.send[m, keep + i, r] + got[m, i, r]

            if stage == self.bits - 1:
                self.mix(layer, m, self.base(self.bits))
        if stage + 1 < self.stages:
            self.start(stage + 1, m)


def transform(mixed_ref, a_ref, iy, m_ref, t_ref):
    owners, each, channels, _ = mixed_ref.shape
    rows, rows2 = a_ref.shape[1], owners * each
    t_step, m_step = rows + PAD, channels + PAD
    for p in range(owners):
        for r in range(each):
            at = pl.ds((p * each + r) * m_step, channels)
            m_ref[at, :] = mixed_ref[p, r].astype(jnp.float32)

    @pl.loop(0, channels // WIDE)
    def _(g):
        for i in range(WIDE):
            c = g * WIDE + i
            part = m_ref[pl.ds(c, rows2, stride=m_step), :].astype(jnp.bfloat16)
            t_ref[pl.ds(c * t_step, rows), :] = dot(a_ref[c], jnp.concatenate([part, iy], axis=0))


def pointwise(w1, w2, rows, t_ref, u_ref, h0_ref, h1_ref, begin=True, end=True):
    steps = rows // (2 * GROUP)
    low, high = (0 if begin else steps // 2), (steps if end else steps // 2)
    channels, t_step = w2.shape[0], rows + PAD
    cg = jnp.bfloat16(GELU_A / GELU_S)

    def expand(base, h_ref):
        parts = [t_ref[pl.ds(base + i, channels, stride=t_step), :] for i in range(GROUP)]
        wide = jnp.concatenate(parts, axis=1).astype(jnp.bfloat16)
        h_ref[...] = dot(w1, wide).astype(jnp.bfloat16)

    def reduce(base, h_ref):
        h = h_ref[...]
        u = dot(w2, h + h * jnp.tanh(h * (h * h + cg)))
        for i in range(GROUP):
            u_ref[pl.ds(base + i, channels, stride=t_step), :] = u[:, i * LANES : (i + 1) * LANES]

    if begin:
        expand(0, h0_ref)

    @pl.loop(low, high)
    def _(g):
        base = g * 2 * GROUP
        expand(base + GROUP, h1_ref)
        reduce(base, h0_ref)
        expand(lax.rem(base + 2 * GROUP, rows), h0_ref)
        reduce(base + GROUP, h1_ref)


def add_update(st_ref, u_ref, c):
    rows = st_ref.shape[1]
    new = st_ref[c].astype(jnp.float32) + u_ref[pl.ds(c * (rows + PAD), rows), :]
    new = new.astype(jnp.bfloat16)
    st_ref[c] = new
    return new


def add_updates(st_ref, u_ref):
    @pl.loop(0, st_ref.shape[0] // 4)
    def _(g):
        for i in range(4):
            add_update(st_ref, u_ref, g * 4 + i)


def scaled_weights(ew, rw):
    w1 = (ew.astype(jnp.float32) * GELU_S).T.astype(jnp.bfloat16)
    return w1, (rw.astype(jnp.float32) * (0.5 / GELU_S)).astype(jnp.bfloat16)


def lanes(m):
    return pl.ds(pl.multiple_of(m * LANES, LANES), LANES)


def tail_kernel(kept, x_ref, mixed_ref, a_hbm, iy_ref, ew_ref, rw_ref, out_ref, *scratch):
    st, mx, a_ref, t_ref, u_ref, h0_ref, h1_ref, m_ref = scratch[:8]
    load_sem, mixed_sem, a_sem, store_sem = scratch[8:]
    chunks, _, rows, _ = st.shape

    def load(m):
        return pltpu.make_async_copy(x_ref.at[:, :, lanes(m)], st.at[m], load_sem.at[m])

    def store(m):
        return pltpu.make_async_copy(st.at[m], out_ref.at[:, :, lanes(m)], store_sem.at[m])

    def mixed(i):
        return pltpu.make_async_copy(mixed_ref.at[i], mx.at[i], mixed_sem.at[i])

    whole_a = pltpu.make_async_copy(a_hbm, a_ref, a_sem)
    whole_a.start()
    for i in range(chunks - kept):
        mixed(i).start()
        load(kept + i).start()
    for m in range(kept):
        load(m).start()
    w1, w2 = scaled_weights(ew_ref[ew_ref.shape[0] - 1], rw_ref[rw_ref.shape[0] - 1])
    whole_a.wait()

    @pl.loop(kept, chunks)
    def _(m):
        mixed(m - kept).wait()
        transform(mx.at[m - kept], a_ref, iy_ref[:, lanes(m)], m_ref, t_ref)
        pointwise(w1, w2, rows, t_ref, u_ref, h0_ref, h1_ref)
        load(m).wait()
        add_updates(st.at[m], u_ref)
        store(m).start()

        @pl.when(m == kept)
        def _():
            for other in range(kept):
                load(other).wait()
                store(other).start()

    @pl.loop(0, chunks)
    def _(m):
        store(m).wait()


def mega(layers, gx, gy, plan, state_ref, fx_ref, fy_ref, ixt_ref, iy_ref, spx_ref, spy_ref,
         ew_ref, rw_ref, out_ref, mixed_out, a_out, *scratch):
    first, later, base, kept = plan
    scratch = list(scratch)
    st, sx, mx, sy, my, t_ref, u_ref, h0_ref, h1_ref, m_ref, acc_ref, a_ref = scratch[:12]
    matx_ref, maty_ref, w1_ref, w2_ref = scratch[12:16]
    bits_x, bits_y = gx.bit_length() - 1, gy.bit_length() - 1
    rx = scratch[16 : 16 + bits_x]
    ry = scratch[16 + bits_x : 16 + bits_x + bits_y]
    sendx, recvx, sendy, recvy, load_sem, store_sem, mixed_sem, a_sem = scratch[16 + bits_x + bits_y :]
    chunks, channels, rows, _ = st.shape
    rows2 = fx_ref.shape[0]
    per_x, per_y = rows2 // gx, rows2 // gy
    t_step, m_step = rows + PAD, channels + PAD
    bf16, f32 = jnp.bfloat16, jnp.float32

    def mix_x(layer, m, at):
        for j in range(per_x // 2):
            pair = sx[m, at, 2 * j : 2 * j + 2].reshape(2 * channels, LANES)
            got = dot(matx_ref[layer, j], pair).astype(bf16)
            mx[m, at, 2 * j : 2 * j + 2] = got.reshape(2, channels, LANES)

    def mix_y(layer, m, at):
        @pl.loop(0, per_y // 2)
        def _(j):
            pair = sy[m, at, pl.ds(2 * j, 2)].reshape(2 * channels, rows)
            got = dot(maty_ref[layer, j], pair).astype(bf16)
            my[m, at, pl.ds(2 * j, 2)] = got.reshape(2, channels, rows)

    ex = Exchange("gx", gx, sx, mx, rx, sendx, recvx, mix_x)
    ey = Exchange("gy", gy, sy, my, ry, sendy, recvy, mix_y)

    def prepare():
        for layer in range(layers):
            w1_ref[layer], w2_ref[layer] = scaled_weights(ew_ref[layer], rw_ref[layer])
            for source, target in ((spx_ref, matx_ref), (spy_ref, maty_ref)):

                @pl.loop(0, source.shape[1])
                def _(j):
                    real, imag = source[layer, j, 0], source[layer, j, 1]
                    target[layer, j, :channels] = jnp.concatenate([real, -imag], axis=1)
                    target[layer, j, channels:] = jnp.concatenate([imag, real], axis=1)

    def load(m):
        return pltpu.make_async_copy(state_ref.at[:, :, lanes(m)], st.at[m], load_sem.at[m])

    def store(m):
        return pltpu.make_async_copy(st.at[m], out_ref.at[:, :, lanes(m)], store_sem.at[m])

    def keep_mixed(i):
        return pltpu.make_async_copy(mx.at[kept + i], mixed_out.at[i], mixed_sem.at[i])

    def keep_a():
        return pltpu.make_async_copy(a_ref, a_out, a_sem)

    def spectra(base, news, fx, fy):
        count = len(news)
        wide = dot(fx, jnp.concatenate(news, axis=1))
        tall = dot_nt(fy, jnp.concatenate(news, axis=0))
        for i in range(count):
            at = pl.ds((base + i) * m_step, rows2)
            m_ref[at, :] = wide[:, i * LANES : (i + 1) * LANES]
            acc_ref[at, :] = acc_ref[at, :] + tall[:, i * rows : (i + 1) * rows]

    def clear(m):
        @pl.when(m == 0)
        def _():
            acc_ref[...] = jnp.zeros_like(acc_ref)

    def send_spectra(m):
        for p in range(gx):
            for r in range(per_x):
                k = p * per_x + r
                sx[m, p, r] = m_ref[pl.ds(k, channels, stride=m_step), :].astype(bf16)
        ex.start(0, m)

        @pl.when(m == chunks - 1)
        def _():
            for p in range(gy):
                for r in range(per_y):
                    k = p * per_y + r
                    sy[0, p, r] = acc_ref[pl.ds(k, channels, stride=m_step), :].astype(bf16)
            if bits_y:
                ey.start(0, 0)

    def first_task(m):
        load(m).wait()
        clear(m)
        fx, fy = fx_ref[...], fy_ref[:, lanes(m)]

        @pl.loop(0, channels // WIDE)
        def _(g):
            base = g * WIDE
            spectra(base, [st[m, base + i] for i in range(WIDE)], fx, fy)

        send_spectra(m)

    def build_a():
        for p in range(gy):
            for r in range(per_y):
                at = pl.ds((p * per_y + r) * m_step, channels)
                acc_ref[at, :] = my[0, p, r].astype(f32)
        top = ixt_ref[...].astype(f32)

        @pl.loop(0, channels // 8)
        def _(g):
            for i in range(8):
                low = acc_ref[pl.ds(g * 8 + i, rows2, stride=m_step), :]
                a_ref[g * 8 + i] = jnp.concatenate([top, low], axis=0).T.astype(bf16)

    def layer_start(layer, m):
        transform(mx.at[m], a_ref, iy_ref[:, lanes(m)], m_ref, t_ref)
        network(layer, end=False)

    def network(layer, **part):
        pointwise(w1_ref[layer], w2_ref[layer], rows, t_ref, u_ref, h0_ref, h1_ref, **part)

    def layer_rest(layer, m):
        network(layer, begin=False)

        @pl.when(layer < layers - 1)
        def _():
            clear(m)
            fx, fy = fx_ref[...], fy_ref[:, lanes(m)]

            @pl.loop(0, channels // WIDE)
            def _(g):
                base = g * WIDE
                spectra(base, [add_update(st.at[m], u_ref, base + i) for i in range(WIDE)], fx, fy)

            send_spectra(m)

        @pl.when((layer == layers - 2) & (m >= kept))
        def _():
            store(m).start()

        @pl.when(layer == layers - 1)
        def _():
            add_updates(st.at[m], u_ref)
            store(m).start()

    barrier = pltpu.get_barrier_semaphore()
    for one in (ex, ey):
        for s in range(one.bits):
            pl.semaphore_signal(
                barrier, inc=1, device_id={one.axis: one.partner(s)}, device_id_type=MESH
            )

    @pl.loop(0, chunks)
    def _(m):
        load(m).start()

    pl.semaphore_wait(barrier, ex.bits + ey.bits)

    ends = stage_ends(ex.stages)

    def place(t, start):
        after = jnp.maximum(t - start, 0)
        turn = jnp.where(t < start, 0, 1 + after // later)
        return turn, jnp.where(t < start, t, lax.rem(after, later))

    @pl.loop(0, first + (layers - 1) * later + kept)
    def _(t):
        turn, m = place(t, first)

        def advance(half):
            for stage in stage_order(ex.stages):
                if ends[stage] % 2 == half:
                    ago = ends[stage] // 2
                    layer, chunk = place(t - ago, base)

                    @pl.when((t >= ago) & (chunk < chunks) & (layer < layers))
                    def _():
                        ex.finish(stage, layer, chunk)
                        if stage == ex.stages - 1:

                            @pl.when((layer == layers - 1) & (chunk >= kept))
                            def _():
                                keep_mixed(chunk - kept).start()

        advance(0)
        for stage in range(ey.stages):
            since = t - first + ey.stages - 1 - stage

            @pl.when((since >= 0) & (lax.rem(jnp.maximum(since, 0), later) == 0))
            def _():
                ey.finish(stage, jnp.maximum(since, 0) // later, 0)

        for i in range(FIRST):

            @pl.when(FIRST * t + i < chunks)
            def _():
                first_task(FIRST * t + i)

        @pl.when((turn > 0) & (m == 0))
        def _():
            build_a()

            @pl.when(turn == layers)
            def _():
                keep_a().start()

        @pl.when((turn > 0) & (m < chunks))
        def _():
            layer_start(turn - 1, m)

        advance(1)

        @pl.when(t == 0)
        def _():
            prepare()

        @pl.when((turn > 0) & (m < chunks))
        def _():
            layer_rest(turn - 1, m)

    @pl.loop(0, chunks)
    def _(m):
        store(m).wait()

    @pl.loop(0, chunks - kept)
    def _(i):
        keep_mixed(i).wait()

    keep_a().wait()


def body(state_field, spectral_x, spectral_y, expand_weight, reduce_weight):
    planes, channels, rows, cols = state_field.shape
    layers, hidden = expand_weight.shape[0], expand_weight.shape[2]
    gx, gy = lax.axis_size("gx"), lax.axis_size("gy")
    nx, ny = rows * gx, cols * gy
    modes = spectral_x.shape[1] * gx
    rows2 = 2 * modes
    chunks = cols // LANES
    bf16, f32 = jnp.bfloat16, jnp.float32
    own_y = spectral_y.shape[1]
    own_x = spectral_x.shape[1]
    forward_x, inverse_x = local_tables(
        lax.axis_index("gx") * rows, rows, nx, mode_order(modes, gx)
    )
    forward_y, inverse_y = local_tables(
        lax.axis_index("gy") * cols, cols, ny, mode_order(modes, gy)
    )

    args = [
        state_field.reshape(channels, rows, cols),
        forward_x,
        forward_y,
        inverse_x,
        inverse_y,
        spectral_x,
        spectral_y,
        expand_weight,
        jnp.swapaxes(reduce_weight, 1, 2),
    ]
    bits_x, bits_y = gx.bit_length() - 1, gy.bit_length() - 1
    per_x, per_y = rows2 // gx, rows2 // gy
    plan = schedule(chunks, 2 * bits_x, 2 * bits_y)
    kept = plan[-1]
    tail = chunks - kept
    m_rows = max(channels, rows2) * (max(channels, rows2) + PAD)
    scratch = [
        pltpu.VMEM((chunks, channels, rows, LANES), bf16),
        pltpu.VMEM((chunks, gx, per_x, channels, LANES), bf16),
        pltpu.VMEM((chunks, gx, per_x, channels, LANES), bf16),
        pltpu.VMEM((1, gy, per_y, channels, rows), bf16),
        pltpu.VMEM((1, gy, per_y, channels, rows), bf16),
        pltpu.VMEM((channels * (rows + PAD), LANES), f32),
        pltpu.VMEM((channels * (rows + PAD), LANES), f32),
        pltpu.VMEM((hidden, GROUP * LANES), bf16),
        pltpu.VMEM((hidden, GROUP * LANES), bf16),
        pltpu.VMEM((m_rows, LANES), f32),
        pltpu.VMEM((m_rows, rows), f32),
        pltpu.VMEM((channels, rows, 2 * rows2), bf16),
        pltpu.VMEM((layers, own_x, 2 * channels, 2 * channels), bf16),
        pltpu.VMEM((layers, own_y, 2 * channels, 2 * channels), bf16),
        pltpu.VMEM((layers, hidden, channels), bf16),
        pltpu.VMEM((layers, channels, hidden), bf16),
    ]
    for s in range(bits_x):
        scratch.append(pltpu.VMEM((chunks, gx >> (s + 1), per_x, channels, LANES), bf16))
    for s in range(bits_y):
        scratch.append(pltpu.VMEM((1, gy >> (s + 1), per_y, channels, rows), bf16))
    dma = pltpu.SemaphoreType.DMA
    scratch += [dma((2 * bits_x, chunks))] * 2 + [dma((2 * bits_y, 1))] * 2 + [dma((chunks,))] * 2
    scratch += [dma((chunks - kept,)), dma(())]
    vmem = pl.BlockSpec(memory_space=pltpu.VMEM)
    anywhere = pl.BlockSpec(memory_space=pl.ANY)
    state_shape = jax.ShapeDtypeStruct((channels, rows, cols), bf16)
    mixed_shape = jax.ShapeDtypeStruct((tail, gx, per_x, channels, LANES), bf16)
    a_shape = jax.ShapeDtypeStruct((channels, rows, 2 * rows2), bf16)
    state, mixed, a = pl.pallas_call(
        functools.partial(mega, layers, gx, gy, plan),
        name="layers",
        out_shape=[state_shape, mixed_shape, a_shape],
        in_specs=[anywhere] + [vmem] * (len(args) - 1),
        out_specs=[anywhere] * 3,
        scratch_shapes=scratch,
        compiler_params=pltpu.CompilerParams(
            collective_id=0, has_side_effects=True, vmem_limit_bytes=67043328
        ),
    )(*args)
    out = pl.pallas_call(
        functools.partial(tail_kernel, kept),
        name="tail",
        out_shape=state_shape,
        in_specs=[anywhere] * 3 + [vmem] * 3,
        out_specs=anywhere,
        scratch_shapes=[
            pltpu.VMEM((chunks, channels, rows, LANES), bf16),
            pltpu.VMEM(mixed_shape.shape, bf16),
            pltpu.VMEM(a_shape.shape, bf16),
            pltpu.VMEM((channels * (rows + PAD), LANES), f32),
            pltpu.VMEM((channels * (rows + PAD), LANES), f32),
            pltpu.VMEM((hidden, GROUP * LANES), bf16),
            pltpu.VMEM((hidden, GROUP * LANES), bf16),
            pltpu.VMEM((m_rows, LANES), f32),
            dma((chunks,)),
            dma((tail,)),
            dma(()),
            dma((chunks,)),
        ],
        compiler_params=pltpu.CompilerParams(vmem_limit_bytes=60 * 1024 * 1024),
    )(state, mixed, a, inverse_y, *args[-2:])
    return out.reshape(state_field.shape)


def solution(mesh):
    in_specs = (
        P(None, None, "gx", "gy"),
        P(None, "gx", None, None, None),
        P(None, "gy", None, None, None),
        P(),
        P(),
    )
    out_specs = P(None, None, "gx", "gy")
    return jax.shard_map(body, mesh=mesh, in_specs=in_specs, out_specs=out_specs, check_vma=False)
```

```python
import functools

import jax
import jax.numpy as jnp
from jax import lax
from jax.experimental import pallas as pl
from jax.experimental.pallas import tpu as pltpu
from jax.sharding import PartitionSpec as P

LANES = 128
PAD = 4
GROUP = 8
FIRST = 2
WIDE = 16
GELU_A = 0.7978845608028654
GELU_B = 0.044715
GELU_S = (GELU_A * GELU_B) ** (1.0 / 3.0)
MESH = pl.DeviceIdType.MESH


def bit_reversed(count):
    bits = count.bit_length() - 1
    return [int(format(i, "b").zfill(bits)[::-1], 2) if bits else 0 for i in range(count)]


def mode_order(modes, owners):
    each = modes // owners
    return [o * each + j for o in bit_reversed(owners) for j in range(each)]


def local_tables(first, count, length, order):
    rows2 = 2 * len(order)
    positions = first + jnp.arange(count, dtype=jnp.int32)
    orders = jnp.array([k for k in order for _ in range(2)], dtype=jnp.int32)[:, None]
    part = lax.broadcasted_iota(jnp.int32, (rows2, count), 0) % 2
    steps = (4 * orders * positions[None, :] + part * length) % (4 * length)
    factor = 1.0 / jnp.sqrt(jnp.float32(length))
    forward = jnp.cos(jnp.pi * steps.astype(jnp.float32) / (2 * length)) * factor
    inverse = jnp.where(orders == 0, 1.0, 2.0) * forward
    return forward.astype(jnp.bfloat16), inverse.astype(jnp.bfloat16)


def dot(left, right):
    return jnp.dot(left, right, preferred_element_type=jnp.float32)


def dot_nt(left, right):
    return lax.dot_general(
        left, right, (((1,), (1,)), ((), ())), preferred_element_type=jnp.float32
    )


def stage_ends(stages):
    spans = [2 if stages >= 4 and s in (1, stages // 2 - 1, stages // 2, stages - 2) else 1 for s in range(stages)]
    return [sum(spans[: s + 1]) for s in range(stages)]


def stage_order(stages):
    if stages < 4:
        return list(reversed(range(stages)))
    first, late = [stages - 1, stages - 3, 0], [stages - 2, 1]
    middle = [s for s in reversed(range(stages)) if s not in first + late]
    return list(dict.fromkeys(first + middle + late))


def schedule(chunks, stages, y_stages):
    late = (stage_ends(stages)[-1] + 1) // 2 if stages else 0
    early = pl.cdiv(chunks, FIRST)
    first = max(late, early + max(y_stages - 1, 0), 1)
    base = max(chunks, first + 1)
    second = max(first + chunks + max(y_stages - 1, 0), base + late + 1)
    kept = min(chunks, max(0, chunks - 2, base + chunks + late - second))
    return first, second - first, base, kept


class Exchange:
    def __init__(self, axis, size, send, full, recv, send_sem, recv_sem, mix):
        self.axis, self.size = axis, size
        self.bits = size.bit_length() - 1
        self.stages = 2 * self.bits
        self.send, self.full, self.recv = send, full, recv
        self.send_sem, self.recv_sem = send_sem, recv_sem
        self.mix = mix
        self.me = lax.axis_index(axis)

    def bit(self, s):
        return lax.rem(self.me // (1 << s), 2)

    def base(self, s):
        total = 0
        for b in range(s):
            total = total + self.bit(b) * (self.size >> (b + 1))
        return total

    def partner(self, s):
        return self.me + (1 - 2 * self.bit(s)) * (1 << s)

    def copy(self, stage, m):
        if stage < self.bits:
            half = self.size >> (stage + 1)
            start = self.base(stage) + (1 - self.bit(stage)) * half
            src = self.send.at[m, pl.ds(start, half)]
            dst = self.recv[stage].at[m]
            peer = self.partner(stage)
        else:
            s = self.stages - 1 - stage
            half = self.size >> (s + 1)
            src = self.full.at[m, pl.ds(self.base(s + 1), half)]
            dst = self.full.at[m, pl.ds(self.base(s + 1), half)]
            peer = self.partner(s)
        return pltpu.make_async_remote_copy(
            src_ref=src,
            dst_ref=dst,
            send_sem=self.send_sem.at[stage, m],
            recv_sem=self.recv_sem.at[stage, m],
            device_id={self.axis: peer},
            device_id_type=MESH,
        )

    def start(self, stage, m):
        self.copy(stage, m).start()

    def finish(self, stage, layer, m):
        self.copy(stage, m).wait()
        if stage < self.bits:
            half = self.size >> (stage + 1)
            keep = self.base(stage + 1)
            rows = self.send.shape[2]
            got = self.recv[stage]

            @pl.loop(0, half)
            def _(i):
                for r in range(rows):
                    self.send[m, keep + i, r] = self.send[m, keep + i, r] + got[m, i, r]

            if stage == self.bits - 1:
                self.mix(layer, m, self.base(self.bits))
        if stage + 1 < self.stages:
            self.start(stage + 1, m)


def transform(mixed_ref, a_ref, iy, m_ref, t_ref):
    owners, each, channels, _ = mixed_ref.shape
    rows, rows2 = a_ref.shape[1], owners * each
    t_step, m_step = rows + PAD, channels + PAD
    for p in range(owners):
        for r in range(each):
            at = pl.ds((p * each + r) * m_step, channels)
            m_ref[at, :] = mixed_ref[p, r].astype(jnp.float32)

    @pl.loop(0, channels // WIDE)
    def _(g):
        for i in range(WIDE):
            c = g * WIDE + i
            part = m_ref[pl.ds(c, rows2, stride=m_step), :].astype(jnp.bfloat16)
            t_ref[pl.ds(c * t_step, rows), :] = dot(a_ref[c], jnp.concatenate([part, iy], axis=0))


def pointwise(w1, w2, rows, t_ref, u_ref, h0_ref, h1_ref, begin=True, end=True):
    steps = rows // (2 * GROUP)
    low, high = (0 if begin else steps // 2), (steps if end else steps // 2)
    channels, t_step = w2.shape[0], rows + PAD
    cg = jnp.bfloat16(GELU_A / GELU_S)

    def expand(base, h_ref):
        parts = [t_ref[pl.ds(base + i, channels, stride=t_step), :] for i in range(GROUP)]
        wide = jnp.concatenate(parts, axis=1).astype(jnp.bfloat16)
        h_ref[...] = dot(w1, wide).astype(jnp.bfloat16)

    def reduce(base, h_ref):
        h = h_ref[...]
        u = dot(w2, h + h * jnp.tanh(h * (h * h + cg)))
        for i in range(GROUP):
            u_ref[pl.ds(base + i, channels, stride=t_step), :] = u[:, i * LANES : (i + 1) * LANES]

    if begin:
        expand(0, h0_ref)

    @pl.loop(low, high)
    def _(g):
        base = g * 2 * GROUP
        expand(base + GROUP, h1_ref)
        reduce(base, h0_ref)
        expand(lax.rem(base + 2 * GROUP, rows), h0_ref)
        reduce(base + GROUP, h1_ref)


def add_update(st_ref, u_ref, c):
    rows = st_ref.shape[1]
    new = st_ref[c].astype(jnp.float32) + u_ref[pl.ds(c * (rows + PAD), rows), :]
    new = new.astype(jnp.bfloat16)
    st_ref[c] = new
    return new


def add_updates(st_ref, u_ref):
    @pl.loop(0, st_ref.shape[0] // 4)
    def _(g):
        for i in range(4):
            add_update(st_ref, u_ref, g * 4 + i)


def scaled_weights(ew, rw):
    w1 = (ew.astype(jnp.float32) * GELU_S).T.astype(jnp.bfloat16)
    return w1, (rw.astype(jnp.float32) * (0.5 / GELU_S)).astype(jnp.bfloat16)


def lanes(m):
    return pl.ds(pl.multiple_of(m * LANES, LANES), LANES)


def tail_kernel(kept, x_ref, mixed_ref, a_hbm, iy_ref, ew_ref, rw_ref, out_ref, *scratch):
    st, mx, a_ref, t_ref, u_ref, h0_ref, h1_ref, m_ref = scratch[:8]
    load_sem, mixed_sem, a_sem, store_sem = scratch[8:]
    chunks, _, rows, _ = st.shape

    def load(m):
        return pltpu.make_async_copy(x_ref.at[:, :, lanes(m)], st.at[m], load_sem.at[m])

    def store(m):
        return pltpu.make_async_copy(st.at[m], out_ref.at[:, :, lanes(m)], store_sem.at[m])

    def mixed(i):
        return pltpu.make_async_copy(mixed_ref.at[i], mx.at[i], mixed_sem.at[i])

    whole_a = pltpu.make_async_copy(a_hbm, a_ref, a_sem)
    whole_a.start()
    for i in range(chunks - kept):
        mixed(i).start()
        load(kept + i).start()
    for m in range(kept):
        load(m).start()
    w1, w2 = scaled_weights(ew_ref[ew_ref.shape[0] - 1], rw_ref[rw_ref.shape[0] - 1])
    whole_a.wait()

    @pl.loop(kept, chunks)
    def _(m):
        mixed(m - kept).wait()
        transform(mx.at[m - kept], a_ref, iy_ref[:, lanes(m)], m_ref, t_ref)
        pointwise(w1, w2, rows, t_ref, u_ref, h0_ref, h1_ref)
        load(m).wait()
        add_updates(st.at[m], u_ref)
        store(m).start()

        @pl.when(m == kept)
        def _():
            for other in range(kept):
                load(other).wait()
                store(other).start()

    @pl.loop(0, chunks)
    def _(m):
        store(m).wait()


def mega(layers, gx, gy, plan, state_ref, fx_ref, fy_ref, ixt_ref, iy_ref, spx_ref, spy_ref,
         ew_ref, rw_ref, out_ref, mixed_out, a_out, *scratch):
    first, later, base, kept = plan
    scratch = list(scratch)
    st, sx, mx, sy, my, t_ref, u_ref, h0_ref, h1_ref, m_ref, acc_ref, a_ref = scratch[:12]
    matx_ref, maty_ref, w1_ref, w2_ref = scratch[12:16]
    bits_x, bits_y = gx.bit_length() - 1, gy.bit_length() - 1
    rx = scratch[16 : 16 + bits_x]
    ry = scratch[16 + bits_x : 16 + bits_x + bits_y]
    sendx, recvx, sendy, recvy, load_sem, store_sem, mixed_sem, a_sem = scratch[16 + bits_x + bits_y :]
    chunks, channels, rows, _ = st.shape
    rows2 = fx_ref.shape[0]
    per_x, per_y = rows2 // gx, rows2 // gy
    t_step, m_step = rows + PAD, channels + PAD
    bf16, f32 = jnp.bfloat16, jnp.float32

    def mix_x(layer, m, at):
        for j in range(per_x // 2):
            pair = sx[m, at, 2 * j : 2 * j + 2].reshape(2 * channels, LANES)
            got = dot(matx_ref[layer, j], pair).astype(bf16)
            mx[m, at, 2 * j : 2 * j + 2] = got.reshape(2, channels, LANES)

    def mix_y(layer, m, at):
        @pl.loop(0, per_y // 2)
        def _(j):
            pair = sy[m, at, pl.ds(2 * j, 2)].reshape(2 * channels, rows)
            got = dot(maty_ref[layer, j], pair).astype(bf16)
            my[m, at, pl.ds(2 * j, 2)] = got.reshape(2, channels, rows)

    ex = Exchange("gx", gx, sx, mx, rx, sendx, recvx, mix_x)
    ey = Exchange("gy", gy, sy, my, ry, sendy, recvy, mix_y)

    def prepare():
        for layer in range(layers):
            w1_ref[layer], w2_ref[layer] = scaled_weights(ew_ref[layer], rw_ref[layer])
            for source, target in ((spx_ref, matx_ref), (spy_ref, maty_ref)):

                @pl.loop(0, source.shape[1])
                def _(j):
                    real, imag = source[layer, j, 0], source[layer, j, 1]
                    target[layer, j, :channels] = jnp.concatenate([real, -imag], axis=1)
                    target[layer, j, channels:] = jnp.concatenate([imag, real], axis=1)

    def load(m):
        return pltpu.make_async_copy(state_ref.at[:, :, lanes(m)], st.at[m], load_sem.at[m])

    def store(m):
        return pltpu.make_async_copy(st.at[m], out_ref.at[:, :, lanes(m)], store_sem.at[m])

    def keep_mixed(i):
        return pltpu.make_async_copy(mx.at[kept + i], mixed_out.at[i], mixed_sem.at[i])

    def keep_a():
        return pltpu.make_async_copy(a_ref, a_out, a_sem)

    def spectra(base, news, fx, fy):
        count = len(news)
        wide = dot(fx, jnp.concatenate(news, axis=1))
        tall = dot_nt(fy, jnp.concatenate(news, axis=0))
        for i in range(count):
            at = pl.ds((base + i) * m_step, rows2)
            m_ref[at, :] = wide[:, i * LANES : (i + 1) * LANES]
            acc_ref[at, :] = acc_ref[at, :] + tall[:, i * rows : (i + 1) * rows]

    def clear(m):
        @pl.when(m == 0)
        def _():
            acc_ref[...] = jnp.zeros_like(acc_ref)

    def send_spectra(m):
        for p in range(gx):
            for r in range(per_x):
                k = p * per_x + r
                sx[m, p, r] = m_ref[pl.ds(k, channels, stride=m_step), :].astype(bf16)
        ex.start(0, m)

        @pl.when(m == chunks - 1)
        def _():
            for p in range(gy):
                for r in range(per_y):
                    k = p * per_y + r
                    sy[0, p, r] = acc_ref[pl.ds(k, channels, stride=m_step), :].astype(bf16)
            if bits_y:
                ey.start(0, 0)

    def first_task(m):
        load(m).wait()
        clear(m)
        fx, fy = fx_ref[...], fy_ref[:, lanes(m)]

        @pl.loop(0, channels // WIDE)
        def _(g):
            base = g * WIDE
            spectra(base, [st[m, base + i] for i in range(WIDE)], fx, fy)

        send_spectra(m)

    def build_a():
        for p in range(gy):
            for r in range(per_y):
                at = pl.ds((p * per_y + r) * m_step, channels)
                acc_ref[at, :] = my[0, p, r].astype(f32)
        top = ixt_ref[...].astype(f32)

        @pl.loop(0, channels // 8)
        def _(g):
            for i in range(8):
                low = acc_ref[pl.ds(g * 8 + i, rows2, stride=m_step), :]
                a_ref[g * 8 + i] = jnp.concatenate([top, low], axis=0).T.astype(bf16)

    def layer_start(layer, m):
        transform(mx.at[m], a_ref, iy_ref[:, lanes(m)], m_ref, t_ref)
        network(layer, end=False)

    def network(layer, **part):
        pointwise(w1_ref[layer], w2_ref[layer], rows, t_ref, u_ref, h0_ref, h1_ref, **part)

    def layer_rest(layer, m):
        network(layer, begin=False)

        @pl.when(layer < layers - 1)
        def _():
            clear(m)
            fx, fy = fx_ref[...], fy_ref[:, lanes(m)]

            @pl.loop(0, channels // WIDE)
            def _(g):
                base = g * WIDE
                spectra(base, [add_update(st.at[m], u_ref, base + i) for i in range(WIDE)], fx, fy)

            send_spectra(m)

        @pl.when((layer == layers - 2) & (m >= kept))
        def _():
            store(m).start()

        @pl.when(layer == layers - 1)
        def _():
            add_updates(st.at[m], u_ref)
            store(m).start()

    barrier = pltpu.get_barrier_semaphore()
    for one in (ex, ey):
        for s in range(one.bits):
            pl.semaphore_signal(
                barrier, inc=1, device_id={one.axis: one.partner(s)}, device_id_type=MESH
            )

    @pl.loop(0, chunks)
    def _(m):
        load(m).start()

    pl.semaphore_wait(barrier, ex.bits + ey.bits)

    ends = stage_ends(ex.stages)

    def place(t, start):
        after = jnp.maximum(t - start, 0)
        turn = jnp.where(t < start, 0, 1 + after // later)
        return turn, jnp.where(t < start, t, lax.rem(after, later))

    @pl.loop(0, first + (layers - 1) * later + kept)
    def _(t):
        turn, m = place(t, first)

        def advance(half):
            for stage in stage_order(ex.stages):
                if ends[stage] % 2 == half:
                    ago = ends[stage] // 2
                    layer, chunk = place(t - ago, base)

                    @pl.when((t >= ago) & (chunk < chunks) & (layer < layers))
                    def _():
                        ex.finish(stage, layer, chunk)
                        if stage == ex.stages - 1:

                            @pl.when((layer == layers - 1) & (chunk >= kept))
                            def _():
                                keep_mixed(chunk - kept).start()

        advance(0)
        for stage in range(ey.stages):
            since = t - first + ey.stages - 1 - stage

            @pl.when((since >= 0) & (lax.rem(jnp.maximum(since, 0), later) == 0))
            def _():
                ey.finish(stage, jnp.maximum(since, 0) // later, 0)

        for i in range(FIRST):

            @pl.when(FIRST * t + i < chunks)
            def _():
                first_task(FIRST * t + i)

        @pl.when((turn > 0) & (m == 0))
        def _():
            build_a()

            @pl.when(turn == layers)
            def _():
                keep_a().start()

        @pl.when((turn > 0) & (m < chunks))
        def _():
            layer_start(turn - 1, m)

        advance(1)

        @pl.when(t == 0)
        def _():
            prepare()

        @pl.when((turn > 0) & (m < chunks))
        def _():
            layer_rest(turn - 1, m)

    @pl.loop(0, chunks)
    def _(m):
        store(m).wait()

    @pl.loop(0, chunks - kept)
    def _(i):
        keep_mixed(i).wait()

    keep_a().wait()


def body(state_field, spectral_x, spectral_y, expand_weight, reduce_weight):
    planes, channels, rows, cols = state_field.shape
    layers, hidden = expand_weight.shape[0], expand_weight.shape[2]
    gx, gy = lax.axis_size("gx"), lax.axis_size("gy")
    nx, ny = rows * gx, cols * gy
    modes = spectral_x.shape[1] * gx
    rows2 = 2 * modes
    chunks = cols // LANES
    bf16, f32 = jnp.bfloat16, jnp.float32
    own_y = spectral_y.shape[1]
    own_x = spectral_x.shape[1]
    forward_x, inverse_x = local_tables(
        lax.axis_index("gx") * rows, rows, nx, mode_order(modes, gx)
    )
    forward_y, inverse_y = local_tables(
        lax.axis_index("gy") * cols, cols, ny, mode_order(modes, gy)
    )

    args = [
        state_field.reshape(channels, rows, cols),
        forward_x,
        forward_y,
        inverse_x,
        inverse_y,
        spectral_x,
        spectral_y,
        expand_weight,
        jnp.swapaxes(reduce_weight, 1, 2),
    ]
    bits_x, bits_y = gx.bit_length() - 1, gy.bit_length() - 1
    per_x, per_y = rows2 // gx, rows2 // gy
    plan = schedule(chunks, 2 * bits_x, 2 * bits_y)
    kept = plan[-1]
    tail = chunks - kept
    m_rows = max(channels, rows2) * (max(channels, rows2) + PAD)
    scratch = [
        pltpu.VMEM((chunks, channels, rows, LANES), bf16),
        pltpu.VMEM((chunks, gx, per_x, channels, LANES), bf16),
        pltpu.VMEM((chunks, gx, per_x, channels, LANES), bf16),
        pltpu.VMEM((1, gy, per_y, channels, rows), bf16),
        pltpu.VMEM((1, gy, per_y, channels, rows), bf16),
        pltpu.VMEM((channels * (rows + PAD), LANES), f32),
        pltpu.VMEM((channels * (rows + PAD), LANES), f32),
        pltpu.VMEM((hidden, GROUP * LANES), bf16),
        pltpu.VMEM((hidden, GROUP * LANES), bf16),
        pltpu.VMEM((m_rows, LANES), f32),
        pltpu.VMEM((m_rows, rows), f32),
        pltpu.VMEM((channels, rows, 2 * rows2), bf16),
        pltpu.VMEM((layers, own_x, 2 * channels, 2 * channels), bf16),
        pltpu.VMEM((layers, own_y, 2 * channels, 2 * channels), bf16),
        pltpu.VMEM((layers, hidden, channels), bf16),
        pltpu.VMEM((layers, channels, hidden), bf16),
    ]
    for s in range(bits_x):
        scratch.append(pltpu.VMEM((chunks, gx >> (s + 1), per_x, channels, LANES), bf16))
    for s in range(bits_y):
        scratch.append(pltpu.VMEM((1, gy >> (s + 1), per_y, channels, rows), bf16))
    dma = pltpu.SemaphoreType.DMA
    scratch += [dma((2 * bits_x, chunks))] * 2 + [dma((2 * bits_y, 1))] * 2 + [dma((chunks,))] * 2
    scratch += [dma((chunks - kept,)), dma(())]
    vmem = pl.BlockSpec(memory_space=pltpu.VMEM)
    anywhere = pl.BlockSpec(memory_space=pl.ANY)
    state_shape = jax.ShapeDtypeStruct((channels, rows, cols), bf16)
    mixed_shape = jax.ShapeDtypeStruct((tail, gx, per_x, channels, LANES), bf16)
    a_shape = jax.ShapeDtypeStruct((channels, rows, 2 * rows2), bf16)
    state, mixed, a = pl.pallas_call(
        functools.partial(mega, layers, gx, gy, plan),
        name="layers",
        out_shape=[state_shape, mixed_shape, a_shape],
        in_specs=[anywhere] + [vmem] * (len(args) - 1),
        out_specs=[anywhere] * 3,
        scratch_shapes=scratch,
        compiler_params=pltpu.CompilerParams(
            collective_id=0, has_side_effects=True, vmem_limit_bytes=67043328
        ),
    )(*args)
    out = pl.pallas_call(
        functools.partial(tail_kernel, kept),
        name="tail",
        out_shape=state_shape,
        in_specs=[anywhere] * 3 + [vmem] * 3,
        out_specs=anywhere,
        scratch_shapes=[
            pltpu.VMEM((chunks, channels, rows, LANES), bf16),
            pltpu.VMEM(mixed_shape.shape, bf16),
            pltpu.VMEM(a_shape.shape, bf16),
            pltpu.VMEM((channels * (rows + PAD), LANES), f32),
            pltpu.VMEM((channels * (rows + PAD), LANES), f32),
            pltpu.VMEM((hidden, GROUP * LANES), bf16),
            pltpu.VMEM((hidden, GROUP * LANES), bf16),
            pltpu.VMEM((m_rows, LANES), f32),
            dma((chunks,)),
            dma((tail,)),
            dma(()),
            dma((chunks,)),
        ],
        compiler_params=pltpu.CompilerParams(vmem_limit_bytes=60 * 1024 * 1024),
    )(state, mixed, a, inverse_y, *args[-2:])
    return out.reshape(state_field.shape)


def solution(mesh):
    in_specs = (
        P(None, None, "gx", "gy"),
        P(None, "gx", None, None, None),
        P(None, "gy", None, None, None),
        P(),
        P(),
    )
    out_specs = P(None, None, "gx", "gy")
    return jax.shard_map(body, mesh=mesh, in_specs=in_specs, out_specs=out_specs, check_vma=False)
```
